32 devices in a mesh: fsdp: 8 (over z, core), seq: 4 (over y, x).
Axes of the slice: x: 2, y: 2, z: 4, core: 2. Of those that a mesh axis runs over, the one named last changes fastest.
Arguments:
- tokens: bfloat16 [16, 1024, 1024], P('fsdp', 'seq'), may hold values from -6 to 6
- segment_ids: int32 [16, 1024], P('fsdp', 'seq'), may hold values from 0 to 3, never falling along the last dimension, each value on 1 to 512 neighbouring positions
- w_qkv: bfloat16 [1024, 3072], P('fsdp'), may hold values from -0.1875 to 0.1875
- w_out: bfloat16 [1024, 1024], P(None, 'fsdp'), may hold values from -1.5 to 1.5
- w_in: bfloat16 [1024, 5248], P('fsdp'), may hold values from -0.1875 to 0.1875
- w_down: bfloat16 [2624, 1024], P(None, 'fsdp'), may hold values from -0.125 to 0.125
- gain_attn: bfloat16 [1024], P('fsdp'), may hold values from 0.5 to 1.5
- gain_mlp: bfloat16 [1024], P('fsdp'), may hold values from 0.5 to 1.5
- grad_output: bfloat16 [16, 1024, 1024], P('fsdp', 'seq'), may hold values from -6 to 6
Outputs:
- output: bfloat16 [16, 1024, 1024], P('fsdp', 'seq')
- grad_tokens: bfloat16 [16, 1024, 1024], P('fsdp', 'seq')
- grad_w_qkv: float32 [1024, 3072], P('fsdp')
- grad_w_out: float32 [1024, 1024], P(None, 'fsdp')
- grad_w_in: float32 [1024, 5248], P('fsdp')
- grad_w_down: float32 [2624, 1024], P(None, 'fsdp')
- grad_gain_attn: float32 [1024], P('fsdp')
- grad_gain_mlp: float32 [1024], P('fsdp')
The draws below stay inside these ranges and needn't reach their ends.
Inputs may be any that keep to these rules, and one draw needn't show every extreme that they name: `segment_ids`: in each sequence the ids never fall; a document is a run of equal ids of 1 to 512 tokens, one of exactly 512.
All inputs are finite; a program needn't handle non-finite values.
Results may differ from the reference program's by a relative error of at most 0.02.
Values may be sent and summed in bfloat16 or wider, within the bound.
No kernel may reach another device: no remote copies, remote signals or barrier semaphores. Data moves between devices by JAX's collectives and lax.ppermute only.
A program may use at most 192 MiB of HBM per device.

```python
import math
import jax
import jax.numpy as jnp
import numpy as np
from jax import lax

D = 1024
HEADS = 16
HD = 64
FF = 2624
LENGTH = 1024
SEQUENCES = 16
DOCS = 4
DOC_MOST = 512


def block_scale(stream_key, shape, split, least, high):
    def one(axis_at, parts):
        heights = jax.random.uniform(jax.random.fold_in(jax.random.fold_in(stream_key, 6), axis_at), (parts,), jnp.float32, least / len(split), high / len(split))
        return jnp.repeat(jnp.exp(heights), shape[axis_at] // parts).reshape((-1,) + (1,) * (len(shape) - axis_at - 1))

    level = one(*split[0])
    for cut in split[1:]:
        level = level * one(*cut)
    return level


def length_profile(number_of, total, bound, skew):
    loads = [(1 << 20) // math.isqrt(rank ** skew) + 1 for rank in range(2, number_of + 1)]
    rest, counts = total - bound - (number_of - 1), [1] * (number_of - 1)
    while rest > 0:
        candidates = [i for i in range(number_of - 1) if counts[i] < bound]
        mass, budget = sum([loads[i] for i in candidates]), rest
        for i in candidates:
            more = min(bound - counts[i], max(1, budget * loads[i] // mass), rest)
            counts[i] = counts[i] + more
            rest = rest - more
    return np.array([bound] + counts)


def uneven(key, amount, total, most, slope):
    if amount == 2:
        one = jax.random.randint(key, (), max(1, total - most), min(most, total - 1) + 1)
        return jnp.stack([one, total - one])
    sizes = jnp.asarray(length_profile(amount, total, most, slope), jnp.int32)
    pairs = (amount - 1) // 2
    giver, taker = sizes[1:1 + 2 * pairs:2], sizes[2:2 + 2 * pairs:2]
    margin = jnp.minimum(giver - 1, most - taker)
    passed = jax.random.randint(jax.random.fold_in(key, 1), (pairs,), 0, 1 << 20) % (margin + 1)
    sizes = sizes.at[1:1 + 2 * pairs:2].set(giver - passed).at[2:2 + 2 * pairs:2].set(taker + passed)
    return sizes[jax.random.permutation(jax.random.fold_in(key, 2), amount)]


def noise(key, dims, width, most, cuts=(), held_as=jnp.bfloat16):
    entries = width * jax.random.normal(key, dims, jnp.float32)
    if cuts:
        entries = entries * block_scale(key, dims, cuts, -0.22, 0.18)
    return jnp.clip(entries, -most, most).astype(held_as)


def setup_inputs(seed: int = 0) -> dict:
    splits = jax.random.split(jax.random.key(seed), 10)
    tokens = noise(splits[0], (SEQUENCES, LENGTH, D), 1.0, 6.0, ((0, 8), (1, 4)))
    segment_ids = jax.vmap(lambda own: jnp.searchsorted(jnp.cumsum(uneven(own, DOCS, LENGTH, DOC_MOST, 2)), jnp.arange(LENGTH), side="right"))(jax.random.split(splits[1], SEQUENCES)).reshape((SEQUENCES, LENGTH)).astype(jnp.int32)
    w_qkv = noise(splits[2], (D, 3 * HEADS * HD), D ** -0.5, 0.1875, ((0, 8),))
    w_out = noise(splits[3], (HEADS * HD, D), (HEADS * HD // 64) ** -0.5, 1.5, ((1, 8),))
    w_in = noise(splits[4], (D, 2 * FF), D ** -0.5, 0.1875, ((0, 8),))
    w_down = noise(splits[5], (FF, D), FF ** -0.5, 0.125, ((1, 8),))
    gain_attn = jnp.clip(1.0 + 0.1 * jax.random.normal(splits[6], (D,), jnp.float32), 0.5, 1.5).astype(jnp.bfloat16)
    gain_mlp = jnp.clip(1.0 + 0.1 * jax.random.normal(splits[7], (D,), jnp.float32), 0.5, 1.5).astype(jnp.bfloat16)
    grad_output = noise(splits[8], (SEQUENCES, LENGTH, D), 1.0, 6.0, ((0, 8), (1, 4)))
    return dict(tokens=tokens, segment_ids=segment_ids, w_qkv=w_qkv, w_out=w_out, w_in=w_in, w_down=w_down, gain_attn=gain_attn, gain_mlp=gain_mlp, grad_output=grad_output)


@jax.custom_vjp
def low(v):
    return lax.optimization_barrier(v.astype(jnp.bfloat16)).astype(jnp.float32)

@jax.custom_vjp
def low_back(v):
    return v

def low_keep(v):
    return (low(v), None)

def low_pass(kept, grad):
    return (grad,)

def back_keep(v):
    return (v, None)

def back_low(kept, grad):
    return (low(grad),)
low.defvjp(low_keep, low_pass)
low_back.defvjp(back_keep, back_low)

def normalize(rows_in, gain):
    center_of = lax.optimization_barrier(jnp.mean(rows_in, axis=-1, keepdims=True))
    centered = rows_in - center_of
    spread = lax.optimization_barrier(jnp.mean(centered * centered, axis=-1, keepdims=True))
    return centered * lax.rsqrt(spread + 1e-05) * gain

def doc_positions(seg_rows):
    places = jnp.arange(seg_rows.shape[1], dtype=jnp.int32)[None, :]
    before = jnp.concatenate([seg_rows[:, :1] - 1, seg_rows[:, :-1]], axis=1)
    begins = jnp.where(seg_rows != before, places, 0)
    return places - lax.cummax(begins, axis=1)

def rope_tables(positions, head_dim):
    half_dim = head_dim // 2
    inverse = jnp.exp(jnp.arange(half_dim, dtype=jnp.float32) * (-2.0 * math.log(160000.0) / head_dim))
    angles = positions.astype(jnp.float32)[..., None] * inverse
    return (jnp.cos(angles), jnp.sin(angles))

def rotate(vector, cosine, sine):
    half_dim = vector.shape[-1] // 2
    first, second = (vector[..., :half_dim], vector[..., half_dim:])
    return jnp.concatenate([first * cosine - second * sine, second * cosine + first * sine], axis=-1)

def gelu_mix(gate_part, up_part):
    return jax.nn.gelu(gate_part, approximate=False) * up_part

def attend(queries, key_rows, values, seg_row):
    length = queries.shape[0]
    block_rows = min(512, length)
    blocks = length // block_rows
    scaling = 1.0 / math.sqrt(HD)

    def one_block(item):
        query_block, seg_block = item
        scores = low_back(jnp.einsum('qhd,khd->hqk', query_block, key_rows, precision=lax.Precision.HIGHEST) * scaling)
        allowed = seg_block[None, :, None] == seg_row[None, None, :]
        scores = jnp.where(allowed, scores, -1e+30)
        shares = low(jax.nn.softmax(scores, axis=-1))
        return jnp.einsum('hqk,khd->qhd', shares, values, precision=lax.Precision.HIGHEST)
    pieces = lax.map(jax.checkpoint(one_block), (queries.reshape(blocks, block_rows, HEADS, HD), seg_row.reshape(blocks, block_rows)))
    return pieces.reshape(length, HEADS, HD)

def layer(rows_in, seg_row, w_qkv, w_out, w_in, w_down, gain_one, gain_two):
    length = rows_in.shape[0]
    positions = doc_positions(seg_row[None, :])[0]
    cosine, sine = rope_tables(positions, HD)
    cosine = cosine[:, None, :]
    sine = sine[:, None, :]
    normed_one = low(normalize(rows_in, gain_one))
    mixed = low_back(jnp.dot(normed_one, w_qkv, precision=lax.Precision.HIGHEST, preferred_element_type=jnp.float32)).reshape(length, HEADS, 3, HD)
    queries = low_back(low(rotate(mixed[:, :, 0], cosine, sine)))
    key_rows = low_back(low(rotate(mixed[:, :, 1], cosine, sine)))
    values = low_back(low(mixed[:, :, 2]))
    context = low_back(low(attend(queries, key_rows, values, seg_row)))
    branch = low_back(jnp.dot(context.reshape(length, HEADS * HD), w_out, precision=lax.Precision.HIGHEST, preferred_element_type=jnp.float32))
    hidden = rows_in + branch
    normed_two = low(normalize(hidden, gain_two))
    gate_up = low_back(jnp.dot(normed_two, w_in, precision=lax.Precision.HIGHEST, preferred_element_type=jnp.float32))
    product = low(gelu_mix(gate_up[:, :FF], gate_up[:, FF:]))
    return hidden + jnp.dot(product, w_down, precision=lax.Precision.HIGHEST, preferred_element_type=jnp.float32)

def reference(tokens, segment_ids, w_qkv, w_out, w_in, w_down, gain_attn, gain_mlp, grad_output):
    params = tuple((item.astype(jnp.float32) for item in (w_qkv, w_out, w_in, w_down, gain_attn, gain_mlp)))

    def per_sequence(carried, item):
        rows_in, seg_row, cotangent = item

        def apply_layer(rows_here, *weights_here):
            return layer(rows_here, seg_row, *weights_here)
        result, pullback = jax.vjp(apply_layer, rows_in.astype(jnp.float32), *params)
        grads = pullback(cotangent.astype(jnp.float32))
        carried = tuple((total + piece for total, piece in zip(carried, grads[1:])))
        return (carried, (result.astype(jnp.bfloat16), grads[0].astype(jnp.bfloat16)))
    initial = tuple((jnp.zeros(item.shape, jnp.float32) for item in params))
    sums, (outputs, input_grads) = lax.scan(per_sequence, initial, (tokens, segment_ids, grad_output))
    return (outputs, input_grads, sums[0], sums[1], sums[2], sums[3], sums[4], sums[5])
```

```python
import functools
import math

import jax
import jax.numpy as jnp
from jax import lax
from jax.experimental import pallas as pl
from jax.experimental.pallas import tpu as pltpu
from jax.sharding import Mesh
from jax.sharding import PartitionSpec as P

D = 1024
HEADS = 16
HD = 64
FF = 2624
SEQ_MB = 1
MICRO = 2


def normalize(rows_in, gain):
    center_of = jnp.mean(rows_in, axis=-1, keepdims=True)
    centered = rows_in - center_of
    spread = jnp.mean(centered * centered, axis=-1, keepdims=True)
    return centered * lax.rsqrt(spread + 1e-05) * gain


def doc_positions(seg_rows):
    places = jnp.arange(seg_rows.shape[1], dtype=jnp.int32)[None, :]
    before = jnp.concatenate([seg_rows[:, :1] - 1, seg_rows[:, :-1]], axis=1)
    begins = jnp.where(seg_rows != before, places, 0)
    return places - lax.cummax(begins, axis=1)


def rope_tables(positions, head_dim):
    half_dim = head_dim // 2
    inverse = jnp.exp(
        jnp.arange(half_dim, dtype=jnp.float32) * (-2.0 * math.log(160000.0) / head_dim)
    )
    angles = positions.astype(jnp.float32)[..., None] * inverse
    return (jnp.cos(angles), jnp.sin(angles))


def rotate(vector, cosine, sine):
    half_dim = vector.shape[-1] // 2
    first, second = (vector[..., :half_dim], vector[..., half_dim:])
    return jnp.concatenate(
        [first * cosine - second * sine, second * cosine + first * sine], axis=-1
    )


def gelu_mix(gate_part, up_part):
    return jax.nn.gelu(gate_part, approximate=False) * up_part


def contract_rows(left, right):
    return lax.dot_general(
        left, right, (((0,), (0,)), ((), ())), preferred_element_type=jnp.float32
    )


def contract_cols(left, right):
    return lax.dot_general(
        left, right, (((1,), (1,)), ((), ())), preferred_element_type=jnp.float32
    )


def fetch(w_qkv, w_out, w_in, w_down, gain_attn, gain_mlp):
    return (
        lax.all_gather(w_qkv, "fsdp", axis=0, tiled=True),
        lax.all_gather(w_out, "fsdp", axis=1, tiled=True),
        lax.all_gather(w_in, "fsdp", axis=0, tiled=True),
        lax.all_gather(w_down, "fsdp", axis=1, tiled=True),
        lax.all_gather(gain_attn, "fsdp", axis=0, tiled=True),
        lax.all_gather(gain_mlp, "fsdp", axis=0, tiled=True),
    )


def attend_forward(queries, key_rows, values, seg_rows, block_rows):
    row_count, length, head_count, head_dim = queries.shape
    scaling = 1.0 / math.sqrt(head_dim)

    def advance(number, carried):
        out_buffer, sums_buffer = carried
        offset = number * block_rows
        query_block = lax.dynamic_slice_in_dim(queries, offset, block_rows, 1)
        seg_block = lax.dynamic_slice_in_dim(seg_rows, offset, block_rows, 1)
        scores = (
            jnp.einsum("rqhd,rkhd->rhqk", query_block, key_rows, preferred_element_type=jnp.float32)
            * scaling
        )
        allowed = seg_block[:, None, :, None] == seg_rows[:, None, None, :]
        scores = jnp.where(allowed, scores, -1e30)
        highest = jnp.max(scores, axis=-1, keepdims=True)
        raised = jnp.exp(scores - highest)
        totals = jnp.sum(raised, axis=-1, keepdims=True)
        shares = (raised / totals).astype(jnp.bfloat16)
        out_block = jnp.einsum(
            "rhqk,rkhd->rqhd", shares, values, preferred_element_type=jnp.float32
        )
        log_block = (highest + jnp.log(totals))[..., 0]
        out_buffer = lax.dynamic_update_slice_in_dim(
            out_buffer, out_block.astype(jnp.bfloat16), offset, 1
        )
        sums_buffer = lax.dynamic_update_slice_in_dim(sums_buffer, log_block, offset, 2)
        return (out_buffer, sums_buffer)

    initial = (
        jnp.zeros(queries.shape, jnp.bfloat16),
        jnp.zeros((row_count, head_count, length), jnp.float32),
    )
    return lax.fori_loop(0, length // block_rows, advance, initial)


def attend_backward(queries, key_rows, values, seg_rows, log_sums, grad_context, block_rows):
    row_count, length, head_count, head_dim = queries.shape
    scaling = 1.0 / math.sqrt(head_dim)

    def advance(number, carried):
        grad_query, grad_key, grad_value = carried
        offset = number * block_rows
        query_block = lax.dynamic_slice_in_dim(queries, offset, block_rows, 1)
        seg_block = lax.dynamic_slice_in_dim(seg_rows, offset, block_rows, 1)
        grad_block = lax.dynamic_slice_in_dim(grad_context, offset, block_rows, 1)
        sums_block = lax.dynamic_slice_in_dim(log_sums, offset, block_rows, 2)
        scores = (
            jnp.einsum("rqhd,rkhd->rhqk", query_block, key_rows, preferred_element_type=jnp.float32)
            * scaling
        )
        allowed = seg_block[:, None, :, None] == seg_rows[:, None, None, :]
        shares = jnp.where(allowed, jnp.exp(scores - sums_block[..., None]), 0.0)
        grad_value = grad_value + jnp.einsum(
            "rhqk,rqhd->rkhd",
            shares.astype(jnp.bfloat16),
            grad_block,
            preferred_element_type=jnp.float32,
        )
        grad_shares = jnp.einsum(
            "rqhd,rkhd->rhqk", grad_block, values, preferred_element_type=jnp.float32
        )
        grad_scores = shares * (grad_shares - jnp.sum(shares * grad_shares, axis=-1, keepdims=True))
        rounded = grad_scores.astype(jnp.bfloat16)
        query_piece = (
            jnp.einsum("rhqk,rkhd->rqhd", rounded, key_rows, preferred_element_type=jnp.float32)
            * scaling
        )
        grad_key = (
            grad_key
            + jnp.einsum(
                "rhqk,rqhd->rkhd", rounded, query_block, preferred_element_type=jnp.float32
            )
            * scaling
        )
        grad_query = lax.dynamic_update_slice_in_dim(
            grad_query, query_piece.astype(jnp.bfloat16), offset, 1
        )
        return (grad_query, grad_key, grad_value)

    initial = (
        jnp.zeros(queries.shape, jnp.bfloat16),
        jnp.zeros(queries.shape, jnp.float32),
        jnp.zeros(queries.shape, jnp.float32),
    )
    grad_query, grad_key, grad_value = lax.fori_loop(0, length // block_rows, advance, initial)
    return (grad_query, grad_key.astype(jnp.bfloat16), grad_value.astype(jnp.bfloat16))


def zero_totals():
    return (
        jnp.zeros((D, 3 * HEADS * HD), jnp.float32),
        jnp.zeros((HEADS * HD, D), jnp.float32),
        jnp.zeros((D, 2 * FF), jnp.float32),
        jnp.zeros((FF, D), jnp.float32),
        jnp.zeros((D,), jnp.float32),
        jnp.zeros((D,), jnp.float32),
    )


def local(tokens, segment_ids, w_qkv, w_out, w_in, w_down, gain_attn, gain_mlp, grad_output):
    seq_devices = lax.axis_size("seq")
    piece_len = tokens.shape[1]
    local_heads = HEADS // seq_devices
    all_ids = lax.all_gather(segment_ids, "seq", axis=1, tiled=True)
    length = all_ids.shape[1]
    block_rows = min(512, length)
    all_positions = doc_positions(all_ids)
    own_positions = lax.dynamic_slice_in_dim(
        all_positions, lax.axis_index("seq") * piece_len, piece_len, 1
    )
    acc_qkv, acc_out, acc_in, acc_down, acc_gain_attn, acc_gain_mlp = zero_totals()
    outputs = []
    input_grads = []
    per_micro = SEQ_MB
    for micro_index in range(MICRO):
        lower = micro_index * per_micro
        upper = lower + per_micro
        gathered = fetch(w_qkv, w_out, w_in, w_down, gain_attn, gain_mlp)
        full_qkv, full_out, full_in, full_down, full_gain_attn, full_gain_mlp = gathered
        gain_one = full_gain_attn.astype(jnp.float32)
        gain_two = full_gain_mlp.astype(jnp.float32)
        rows_in = tokens[lower:upper].astype(jnp.float32).reshape(-1, D)
        low_one = normalize(rows_in, gain_one).astype(jnp.bfloat16)
        mixed = jnp.dot(low_one, full_qkv, preferred_element_type=jnp.float32).reshape(
            per_micro, piece_len, HEADS, 3, HD
        )
        cosine, sine = rope_tables(own_positions[lower:upper], HD)
        cosine = cosine[:, :, None, :]
        sine = sine[:, :, None, :]
        stacked = jnp.stack(
            [
                rotate(mixed[:, :, :, 0], cosine, sine),
                rotate(mixed[:, :, :, 1], cosine, sine),
                mixed[:, :, :, 2],
            ],
            axis=3,
        )
        stacked = stacked.astype(jnp.bfloat16).reshape(per_micro, piece_len, HEADS * 3 * HD)
        head_side = lax.all_to_all(stacked, "seq", split_axis=2, concat_axis=1, tiled=True).reshape(
            per_micro, length, local_heads, 3, HD
        )
        queries = head_side[:, :, :, 0]
        key_rows = head_side[:, :, :, 1]
        values = head_side[:, :, :, 2]
        ids_micro = all_ids[lower:upper]
        attended, log_sums = attend_forward(queries, key_rows, values, ids_micro, block_rows)
        token_side = lax.all_to_all(
            attended.reshape(per_micro, length, local_heads * HD),
            "seq",
            split_axis=1,
            concat_axis=2,
            tiled=True,
        )
        context = token_side.reshape(-1, HEADS * HD)
        hidden = rows_in + jnp.dot(context, full_out, preferred_element_type=jnp.float32)
        low_two = normalize(hidden, gain_two).astype(jnp.bfloat16)
        gate_up = jnp.dot(low_two, full_in, preferred_element_type=jnp.float32)
        gate_part = gate_up[:, :FF]
        up_part = gate_up[:, FF:]
        product = gelu_mix(gate_part, up_part).astype(jnp.bfloat16)
        result = hidden + jnp.dot(product, full_down, preferred_element_type=jnp.float32)
        outputs.append(result.astype(jnp.bfloat16).reshape(per_micro, piece_len, D))
        grad_rows = grad_output[lower:upper].reshape(-1, D)
        acc_down = acc_down + contract_rows(product, grad_rows)
        grad_product = contract_cols(grad_rows, full_down)
        unused_mix, pull_mix = jax.vjp(gelu_mix, gate_part, up_part)
        grad_gate, grad_up = pull_mix(grad_product)
        grad_gate_up = jnp.concatenate([grad_gate, grad_up], axis=1).astype(jnp.bfloat16)
        acc_in = acc_in + contract_rows(low_two, grad_gate_up)
        grad_normed_two = contract_cols(grad_gate_up, full_in)
        unused_two, pull_two = jax.vjp(normalize, hidden, gain_two)
        grad_hidden_part, grad_gain_two = pull_two(grad_normed_two)
        acc_gain_mlp = acc_gain_mlp + grad_gain_two
        grad_hidden = grad_rows.astype(jnp.float32) + grad_hidden_part
        grad_branch = grad_hidden.astype(jnp.bfloat16)
        acc_out = acc_out + contract_rows(context, grad_branch)
        grad_context = (
            contract_cols(grad_branch, full_out)
            .astype(jnp.bfloat16)
            .reshape(per_micro, piece_len, HEADS * HD)
        )
        grad_heads = lax.all_to_all(
            grad_context, "seq", split_axis=2, concat_axis=1, tiled=True
        ).reshape(per_micro, length, local_heads, HD)
        grad_query, grad_key, grad_value = attend_backward(
            queries, key_rows, values, ids_micro, log_sums, grad_heads, block_rows
        )
        grad_stack = jnp.stack([grad_query, grad_key, grad_value], axis=3).reshape(
            per_micro, length, local_heads * 3 * HD
        )
        grad_tok_side = (
            lax.all_to_all(grad_stack, "seq", split_axis=1, concat_axis=2, tiled=True)
            .reshape(per_micro, piece_len, HEADS, 3, HD)
            .astype(jnp.float32)
        )
        grad_mixed = jnp.stack(
            [
                rotate(grad_tok_side[:, :, :, 0], cosine, -sine),
                rotate(grad_tok_side[:, :, :, 1], cosine, -sine),
                grad_tok_side[:, :, :, 2],
            ],
            axis=3,
        )
        grad_mixed = grad_mixed.astype(jnp.bfloat16).reshape(-1, 3 * HEADS * HD)
        acc_qkv = acc_qkv + contract_rows(low_one, grad_mixed)
        grad_normed_one = contract_cols(grad_mixed, full_qkv)
        unused_one, pull_one = jax.vjp(normalize, rows_in, gain_one)
        grad_input_part, grad_gain_one = pull_one(grad_normed_one)
        acc_gain_attn = acc_gain_attn + grad_gain_one
        input_grads.append(
            (grad_hidden + grad_input_part).astype(jnp.bfloat16).reshape(per_micro, piece_len, D)
        )
    totals = (acc_qkv, acc_out, acc_in, acc_down, acc_gain_attn, acc_gain_mlp)
    shards = (
        lax.psum_scatter(
            totals[0].astype(jnp.bfloat16), "fsdp", scatter_dimension=0, tiled=True
        ).astype(jnp.float32),
        lax.psum_scatter(
            totals[1].astype(jnp.bfloat16), "fsdp", scatter_dimension=1, tiled=True
        ).astype(jnp.float32),
        lax.psum_scatter(
            totals[2].astype(jnp.bfloat16), "fsdp", scatter_dimension=0, tiled=True
        ).astype(jnp.float32),
        lax.psum_scatter(
            totals[3].astype(jnp.bfloat16), "fsdp", scatter_dimension=1, tiled=True
        ).astype(jnp.float32),
        lax.psum_scatter(
            totals[4].astype(jnp.bfloat16), "fsdp", scatter_dimension=0, tiled=True
        ).astype(jnp.float32),
        lax.psum_scatter(
            totals[5].astype(jnp.bfloat16), "fsdp", scatter_dimension=0, tiled=True
        ).astype(jnp.float32),
    )
    owned = (
        lax.psum(shards[0].astype(jnp.bfloat16), "seq").astype(jnp.float32),
        lax.psum(shards[1].astype(jnp.bfloat16), "seq").astype(jnp.float32),
        lax.psum(shards[2].astype(jnp.bfloat16), "seq").astype(jnp.float32),
        lax.psum(shards[3].astype(jnp.bfloat16), "seq").astype(jnp.float32),
        lax.psum(shards[4].astype(jnp.bfloat16), "seq").astype(jnp.float32),
        lax.psum(shards[5].astype(jnp.bfloat16), "seq").astype(jnp.float32),
    )
    return (
        jnp.concatenate(outputs, axis=0),
        jnp.concatenate(input_grads, axis=0),
        owned[0],
        owned[1],
        owned[2],
        owned[3],
        owned[4],
        owned[5],
    )


def spread(mesh):
    return jax.shard_map(
        local,
        mesh=mesh,
        in_specs=(
            P("fsdp", "seq", None),
            P("fsdp", "seq"),
            P("fsdp", None),
            P(None, "fsdp"),
            P("fsdp", None),
            P(None, "fsdp"),
            P("fsdp"),
            P("fsdp"),
            P("fsdp", "seq", None),
        ),
        out_specs=(
            P("fsdp", "seq", None),
            P("fsdp", "seq", None),
            P("fsdp", None),
            P(None, "fsdp"),
            P("fsdp", None),
            P(None, "fsdp"),
            P("fsdp"),
            P("fsdp"),
        ),
        check_vma=False,
    )


F32 = jnp.float32
BF16 = jnp.bfloat16
NN = (((1,), (0,)), ((), ()))
NT = (((1,), (1,)), ((), ()))
TN = (((0,), (0,)), ((), ()))
MIB = 1 << 20
LANES = 128
HALF = HD // 2
PAIR = 2
QKV = 3 * PAIR * HD
OUT = PAIR * HD
UNITS = FF // 8
HIDDEN = -(-UNITS // 16) * 16
EXTRA = 16
TILE = 256
BOTH = [(0, 1), (1, 0)]


def mul(left, right, dims):
    return lax.dot_general(left, right, dims, preferred_element_type=F32)


def whole_in_vmem(count):
    return [pl.BlockSpec(memory_space=pltpu.VMEM)] * count


def lay_flat(flat_ref, blocks_ref, start, count, to=0):
    for k in range(blocks_ref.shape[0]):
        flat_ref[to : to + count, LANES * k : LANES * (k + 1)] = blocks_ref[k, start : start + count, :]


def mlp_body(first, n_ref, dy_ref, w_ref, *rest):
    if first:
        y_ref, dn_ref, ga_ref, gb_ref, w_all, acc = rest
    else:
        y_in, dn_in, y_ref, dn_ref, ga_ref, gb_ref, w_all, acc = rest
    step = pl.program_id(0)

    @pl.when(step == 0)
    def _():
        lay_flat(w_all, w_ref, OUT, 3 * HIDDEN)

    n_t = n_ref[...]
    dy_t = dy_ref[...]
    gate = mul(w_all[0:HIDDEN, :], n_t, NT)
    up = mul(w_all[HIDDEN : 2 * HIDDEN, :], n_t, NT)
    dm = mul(w_all[2 * HIDDEN :, :], dy_t, NT)
    phi = 0.5 * (1.0 + lax.erf(gate * math.sqrt(0.5)))
    gelu = gate * phi
    slope = phi + gate * (jnp.exp(-0.5 * gate * gate) * (1.0 / math.sqrt(2.0 * math.pi)))
    mix = (gelu * up).astype(BF16)
    dgu = jnp.concatenate([dm * up * slope, dm * gelu], axis=0).astype(BF16)
    y = mul(mix, w_all[2 * HIDDEN :, :], TN)
    dn = mul(dgu, w_all[0 : 2 * HIDDEN, :], TN)
    if first:
        y_ref[...] = y
        dn_ref[...] = dn
    else:
        y_ref[...] = y_in[...] + y
        dn_ref[...] = dn_in[...] + dn
    g_in = mul(dgu, n_t, NN)
    g_down = mul(mix, dy_t, NN)

    @pl.when(step == 0)
    def _():
        acc[0 : 2 * HIDDEN, :] = g_in
        acc[2 * HIDDEN :, :] = g_down

    @pl.when(step != 0)
    def _():
        acc[0 : 2 * HIDDEN, :] += g_in
        acc[2 * HIDDEN :, :] += g_down

    @pl.when(step == pl.num_programs(0) - 1)
    def _():
        half = ga_ref.shape[0]
        for k in range(half):
            ga_ref[k] = acc[:, LANES * k : LANES * (k + 1)].astype(BF16)
            gb_ref[k] = acc[:, LANES * (k + half) : LANES * (k + half + 1)].astype(BF16)


def mlp(n2, dy, weights, sums):
    first = sums is None
    tokens, width = n2.shape
    blocks, rows, lanes = weights.shape
    row_tile = pl.BlockSpec((TILE, width), lambda t: (t, 0))
    half = pl.BlockSpec((blocks // 2, 3 * HIDDEN, lanes), lambda t: (0, 0, 0))
    total = jax.ShapeDtypeStruct((tokens, width), F32)
    grads = jax.ShapeDtypeStruct((blocks // 2, 3 * HIDDEN, lanes), BF16)
    y, dn, ga, gb = pl.pallas_call(
        functools.partial(mlp_body, first),
        grid=(tokens // TILE,),
        in_specs=[row_tile, row_tile, pl.BlockSpec(weights.shape, lambda t: (0, 0, 0))]
        + ([] if first else [row_tile, row_tile]),
        out_specs=[row_tile, row_tile, half, half],
        out_shape=[total, total, grads, grads],
        scratch_shapes=[pltpu.VMEM((3 * HIDDEN, width), BF16), pltpu.VMEM((3 * HIDDEN, width), F32)],
        input_output_aliases={} if first else {3: 0, 4: 1},
        compiler_params=pltpu.CompilerParams(vmem_limit_bytes=40 * MIB),
        cost_estimate=pl.CostEstimate(
            flops=18 * tokens * HIDDEN * width,
            transcendentals=2 * tokens * HIDDEN,
            bytes_accessed=20 * tokens * width + 12 * HIDDEN * width,
        ),
        name="mlp",
    )(*([n2, dy, weights] + ([] if first else list(sums))))
    return (y, dn), (ga, gb)


def lane_group(shape, width):
    return (lax.broadcasted_iota(jnp.int32, shape, 1) // width) % 2


def forward_body(n_ref, w_ref, cos_ref, sin_ref, row_ref, col_ref, q_ref, k_ref, v_ref, o_ref, lse_ref, w_all):
    tokens = n_ref.shape[0]
    lay_flat(w_all, w_ref, 0, QKV)

    def project(i, carry):
        here = pl.ds(pl.multiple_of(i * TILE, TILE), TILE)
        mixed = mul(n_ref[here, :], w_all[...], NT)
        cosine, sine = cos_ref[here, :], sin_ref[here, :]
        query, key = mixed[:, 0:OUT], mixed[:, OUT : 2 * OUT]
        q_ref[here, :] = (query * cosine + pltpu.roll(query, HD, 1) * sine).astype(BF16)
        k_ref[here, :] = (key * cosine + pltpu.roll(key, HD, 1) * sine).astype(BF16)
        v_ref[here, :] = mixed[:, 2 * OUT :].astype(BF16)
        return carry

    lax.fori_loop(0, tokens // TILE, project, 0)

    def attend(i, carry):
        here = pl.ds(pl.multiple_of(i * TILE, TILE), TILE)
        query = q_ref[here, :]
        allowed = col_ref[here, 0:1] == row_ref[0:1, :]
        pair = lane_group((TILE, OUT), HALF)
        outs, sums = [], []
        for head in range(PAIR):
            masked = jnp.where(pair == head, query, jnp.zeros_like(query))
            scores = mul(masked, k_ref[...], NT) * (1.0 / math.sqrt(HD))
            scores = jnp.where(allowed, scores, -1e30)
            top = jnp.max(scores, axis=1, keepdims=True)
            raised = jnp.exp(scores - top)
            total = jnp.sum(raised, axis=1, keepdims=True)
            outs.append(mul(raised.astype(BF16), v_ref[...], NN) / total)
            sums.append(top + jnp.log(total))
        side = lane_group((TILE, OUT), HD)
        o_ref[here, :] = jnp.where(side == 0, outs[0], outs[1]).astype(BF16)
        lane = lax.broadcasted_iota(jnp.int32, (TILE, LANES), 1)
        both = jnp.where(lane == 0, sums[0], sums[1])
        lse_ref[:, here] = both.T[0:8, :]
        return carry

    lax.fori_loop(0, tokens // TILE, attend, 0)


def attention(n1, weights, tables):
    tokens, width = n1.shape
    return pl.pallas_call(
        forward_body,
        in_specs=whole_in_vmem(6),
        out_specs=whole_in_vmem(5),
        out_shape=[jax.ShapeDtypeStruct((tokens, OUT), BF16)] * 4 + [jax.ShapeDtypeStruct((8, tokens), F32)],
        scratch_shapes=[pltpu.VMEM((QKV, width), BF16)],
        compiler_params=pltpu.CompilerParams(vmem_limit_bytes=32 * MIB),
        cost_estimate=pl.CostEstimate(
            flops=2 * tokens * QKV * width + 8 * tokens * tokens * OUT,
            transcendentals=2 * tokens * tokens,
            bytes_accessed=6 * MIB,
        ),
        name="attention",
    )(n1, weights, *tables)


def backward_body(
    q_ref, k_ref, v_ref, o_ref, lse_ref, da_ref, n_ref, w_ref, cos_ref, sin_ref, row_ref, col_ref,
    d_ref, ga_ref, gb_ref, w_all, do_ref, dq_ref, dk_ref, dv_ref,
):
    tokens = n_ref.shape[0]
    scaling = 1.0 / math.sqrt(HD)
    lay_flat(w_all, w_ref, 0, OUT)
    do_ref[...] = mul(da_ref[...], w_all[...], NT).astype(BF16)
    dk_ref[...] = jnp.zeros_like(dk_ref)
    dv_ref[...] = jnp.zeros_like(dv_ref)

    def step(i, carry):
        here = pl.ds(pl.multiple_of(i * TILE, TILE), TILE)
        query, grad = q_ref[here, :], do_ref[here, :]
        allowed = col_ref[:, 0:1] == row_ref[0:1, here]
        pair = lane_group((TILE, OUT), HALF)
        side = lane_group((TILE, OUT), HD)
        pair_all = lane_group((tokens, OUT), HALF)
        dq = jnp.zeros((TILE, OUT), F32)
        for head in range(PAIR):
            q_m = jnp.where(pair == head, query, jnp.zeros_like(query))
            g_m = jnp.where(side == head, grad, jnp.zeros_like(grad))
            k_m = jnp.where(pair_all == head, k_ref[...], jnp.zeros_like(k_ref))
            scores = mul(k_ref[...], q_m, NT) * scaling
            share = jnp.exp(jnp.where(allowed, scores - lse_ref[head : head + 1, here], -1e30))
            dshare = mul(v_ref[...], g_m, NT)
            delta = jnp.sum(share * dshare, axis=0, keepdims=True)
            ds = (share * (dshare - delta)).astype(BF16)
            dv_ref[...] += mul(share.astype(BF16), g_m, NN)
            dk_ref[...] += mul(ds, q_m, NN)
            dq += mul(ds, k_m, TN)
        dq_ref[here, :] = dq
        return carry

    lax.fori_loop(0, tokens // TILE, step, 0)
    cosine, sine = cos_ref[...], sin_ref[...]
    dq = (dq_ref[...] * scaling).astype(BF16).astype(F32)
    dk = (dk_ref[...] * scaling).astype(BF16).astype(F32)
    d_ref[:, 0:OUT] = (dq * cosine - pltpu.roll(dq, HD, 1) * sine).astype(BF16)
    d_ref[:, OUT : 2 * OUT] = (dk * cosine - pltpu.roll(dk, HD, 1) * sine).astype(BF16)
    d_ref[:, 2 * OUT :] = dv_ref[...].astype(BF16)
    half = ga_ref.shape[0]
    for k in range(half):
        for ref, at in ((ga_ref, k), (gb_ref, k + half)):
            lanes = slice(LANES * at, LANES * (at + 1))
            ref[k, 0:QKV, :] = mul(d_ref[...], n_ref[:, lanes], TN).astype(BF16)
            ref[k, QKV:, :] = mul(o_ref[...], da_ref[:, lanes], TN).astype(BF16)


def attention_back(saved, dattn, n1, rest, tables):
    tokens, width = n1.shape
    blocks = rest.shape[0]
    vmem = pl.BlockSpec(memory_space=pltpu.VMEM)
    grads = jax.ShapeDtypeStruct((blocks // 2, QKV + OUT, LANES), BF16)
    return pl.pallas_call(
        backward_body,
        grid=(1,),
        in_specs=[vmem] * 7 + [pl.BlockSpec((blocks, OUT, LANES), lambda i: (0, 0, 0))] + [vmem] * 4,
        out_specs=whole_in_vmem(3),
        out_shape=[jax.ShapeDtypeStruct((tokens, QKV), BF16), grads, grads],
        scratch_shapes=[pltpu.VMEM((OUT, width), BF16), pltpu.VMEM((tokens, OUT), BF16)]
        + [pltpu.VMEM((tokens, OUT), F32)] * 3,
        compiler_params=pltpu.CompilerParams(vmem_limit_bytes=40 * MIB),
        cost_estimate=pl.CostEstimate(
            flops=2 * tokens * width * (QKV + 2 * OUT) + 20 * tokens * tokens * OUT,
            transcendentals=2 * tokens * tokens,
            bytes_accessed=10 * MIB,
        ),
        name="attention_back",
    )(*saved, dattn, n1, rest, *tables)


def gather_body(count, *refs):
    lefts, weights = refs[:count], refs[count : 2 * count]
    own_ref, other_ref, w_all = refs[2 * count :]
    inner = lefts[0].shape[1]
    step = pl.program_id(0)
    steps = pl.num_programs(0)

    @pl.when(step == 0)
    def _():
        for r in range(count):
            lay_flat(w_all, weights[r], 0, inner, r * inner)

    rows = jnp.concatenate([left[...] for left in lefts], axis=1)
    total = mul(rows, w_all[...], NN)

    @pl.when(step < steps // 2)
    def _():
        own_ref[...] = total

    @pl.when(step >= steps // 2)
    def _():
        other_ref[...] = total.astype(BF16)


def partial_rows(lefts, weights):
    count = len(lefts)
    tokens, inner = lefts[0].shape
    blocks = weights[0].shape[0]
    width = blocks * LANES
    steps = tokens // TILE
    return pl.pallas_call(
        functools.partial(gather_body, count),
        grid=(steps,),
        in_specs=[pl.BlockSpec((TILE, inner), lambda t: (t, 0))] * count
        + [pl.BlockSpec((blocks, inner, LANES), lambda t: (0, 0, 0))] * count,
        out_specs=[
            pl.BlockSpec((TILE, width), lambda t: (jnp.minimum(t, steps // 2 - 1), 0)),
            pl.BlockSpec((TILE, width), lambda t: (jnp.maximum(t - steps // 2, 0), 0)),
        ],
        out_shape=[
            jax.ShapeDtypeStruct((tokens // 2, width), F32),
            jax.ShapeDtypeStruct((tokens // 2, width), BF16),
        ],
        scratch_shapes=[pltpu.VMEM((count * inner, width), BF16)],
        compiler_params=pltpu.CompilerParams(vmem_limit_bytes=40 * MIB),
        cost_estimate=pl.CostEstimate(
            flops=2 * tokens * count * inner * width, transcendentals=0, bytes_accessed=8 * MIB
        ),
        name="partial_rows",
    )(*lefts, *weights)


def swap(value, axis):
    return lax.ppermute(value, axis, BOTH)


def plane_pairs():
    near, far = [], []
    for c in range(2):
        for y in range(2):
            for x in range(2):
                at = 4 * c + 2 * y + x
                if c == y:
                    near.append((at, 4 * c + 2 * y + 1 - x))
                else:
                    near.append((at, 4 * y + 2 * (1 - y) + x))
                    far.append((at, 4 * y + 2 * (1 - y) + 1 - x))
    return near, far


def to_sequence(local_rows, straight, x):
    near, far = plane_pairs()
    first, second = local_rows[0], local_rows[1]
    same = jnp.where(x == 0, first, second)
    other = jnp.where(x == 0, second, first)
    got_near = lax.ppermute(jnp.where(straight, other, same), ("c", "y", "x"), near)
    got_far = lax.ppermute(other, ("c", "y", "x"), far)
    return jnp.where(straight, same, got_near), jnp.where(straight, got_near, got_far)


def from_sequence(rows, straight, x):
    near, far = plane_pairs()
    piece = rows.shape[0] // 2
    first, second = rows[:piece], rows[piece:]
    got_near = lax.ppermute(jnp.where(straight, second, first), ("c", "y", "x"), near)
    got_far = lax.ppermute(second, ("c", "y", "x"), far)
    same = jnp.where(straight, first, got_near)
    other = jnp.where(straight, got_near, got_far)
    return jnp.where(x == 0, jnp.stack([same, other]), jnp.stack([other, same]))


def moments(rows):
    center = jnp.mean(rows, axis=-1, keepdims=True)
    shifted = rows - center
    scale = lax.rsqrt(jnp.mean(shifted * shifted, axis=-1, keepdims=True) + 1e-05)
    return shifted * scale, scale


def norm_back(grad, gain, normed, scale):
    scaled = grad * gain
    pulled = scaled - jnp.mean(scaled, axis=-1, keepdims=True)
    pulled = pulled - normed * jnp.mean(scaled * normed, axis=-1, keepdims=True)
    return pulled * scale, jnp.sum(grad * normed, axis=0)


def plane_gather(own):
    half = own.shape[0] // 2
    across = swap(own, "x")
    along = swap(own, "y")
    corner = jnp.concatenate([swap(along[:half], "x"), swap(across[half:], "y")], axis=0)
    return [own, across, along, corner]


def add_low(left, right):
    return (left.astype(F32) + right.astype(F32)).astype(BF16)


def plane_reduce(parts):
    a = [part[0] for part in parts]
    b = [part[1] for part in parts]
    here_a = add_low(a[0], swap(a[1], "x"))
    next_a = add_low(a[2], swap(a[3], "x"))
    here_b = add_low(b[0], swap(b[2], "y"))
    next_b = add_low(b[1], swap(b[3], "y"))
    return add_low(here_a, swap(next_a, "y")), add_low(here_b, swap(next_b, "x"))


def in_order(parts, x, y, c):
    stacked = jnp.stack(parts)
    stacked = jnp.where(x == 0, stacked, stacked[jnp.array([1, 0, 3, 2])])
    stacked = jnp.where(y == 0, stacked, stacked[jnp.array([2, 3, 0, 1])])
    return jnp.where(c == 0, stacked, stacked[:, ::-1])


def owned_gradient(total, c):
    mine = lax.psum_scatter(total, "z", scatter_dimension=0, tiled=True)
    keep = lax.dynamic_index_in_dim(mine, c, 0, keepdims=False)
    give = lax.dynamic_index_in_dim(mine, 1 - c, 0, keepdims=False)
    own = jnp.stack([keep, swap(give, "c")])
    corner = lax.ppermute(own, ("y", "x"), [(0, 3), (1, 2), (2, 1), (3, 0)])
    return [own, swap(own, "x"), swap(own, "y"), corner]


def spread_pieces(pieces, c):
    keep = lax.dynamic_index_in_dim(pieces, c, 0, keepdims=False)
    give = lax.dynamic_index_in_dim(pieces, 1 - c, 0, keepdims=False)
    got = swap(give, "c")
    both = jnp.where(c == 0, jnp.stack([keep, got]), jnp.stack([got, keep]))
    return lax.all_gather(both, "z", axis=0, tiled=True)


def chip_local(tokens, segment_ids, w_qkv, w_out, w_in, w_down, gain_attn, gain_mlp, grad_output):
    c, y, x = lax.axis_index("c"), lax.axis_index("y"), lax.axis_index("x")
    place = 2 * y + x
    straight = c == y
    piece = tokens.shape[1]

    qkv = lax.dynamic_index_in_dim(w_qkv.reshape(LANES, 2, 4, QKV), place, 2, keepdims=False)
    qkv = qkv.reshape(LANES, 2, PAIR, 3, 2, HALF)
    qk = qkv[:, :, :, 0:2].transpose(1, 3, 4, 2, 5, 0).reshape(2, 2 * OUT, LANES)
    val = qkv[:, :, :, 2].transpose(1, 2, 3, 4, 0).reshape(2, OUT, LANES)
    gains = jnp.broadcast_to(jnp.stack([gain_attn, gain_mlp])[None], (2, 2, LANES))
    gains = jnp.concatenate([gains, jnp.zeros((2, EXTRA - 2, LANES), BF16)], axis=1)
    first_pieces = jnp.concatenate([qk, val, gains], axis=1)
    out_rows = lax.dynamic_index_in_dim(w_out.reshape(2, 4, OUT, LANES), place, 1, keepdims=False)
    down_rows = lax.dynamic_index_in_dim(w_down.reshape(2, 4, UNITS, LANES), place, 1, keepdims=False)
    in_rows = lax.dynamic_index_in_dim(w_in.T.reshape(2, 2, 4, UNITS, LANES), place, 2, keepdims=False)
    fill = ((0, 0), (0, HIDDEN - UNITS), (0, 0))
    rest_pieces = jnp.concatenate(
        [out_rows, jnp.pad(in_rows[0], fill), jnp.pad(in_rows[1], fill), jnp.pad(down_rows, fill)], axis=1
    )
    qkv_own = spread_pieces(first_pieces, c)
    rest_own = spread_pieces(rest_pieces, c)
    gain_one = qkv_own[:, QKV, :].reshape(1, D).astype(F32)
    gain_two = qkv_own[:, QKV + 1, :].reshape(1, D).astype(F32)

    ids_row = jnp.pad(segment_ids.astype(BF16)[:, None, :], ((0, 0), (0, 7), (0, D - piece)))
    first, second = to_sequence(jnp.concatenate([tokens, ids_row], axis=1), straight, x)
    rows_in = jnp.concatenate([first[:piece], second[:piece]], axis=0).astype(F32)
    own_ids = jnp.concatenate([first[piece : piece + 1, :piece], second[piece : piece + 1, :piece]], axis=1)
    ids = jnp.concatenate([own_ids, swap(own_ids, "c")], axis=1).astype(F32)
    dy_first, dy_second = to_sequence(grad_output, straight, x)
    dy_own = jnp.concatenate([dy_first, dy_second], axis=0)
    dy = jnp.concatenate([dy_own, swap(dy_own, "c")], axis=0)

    order = jnp.stack([2 * c + x, 2 * c + 1 - x, 2 * (1 - c) + x, 2 * (1 - c) + 1 - x])
    places = (order[:, None] * piece + jnp.arange(piece)[None, :]).reshape(-1)
    begins = jnp.sum((ids < ids.reshape(-1, 1)).astype(F32), axis=1)
    cosine, sine = rope_tables(places.astype(F32) - begins, HD)
    cosine = jnp.concatenate([cosine] * 4, axis=1)
    sine = jnp.concatenate([-sine, -sine, sine, sine], axis=1)
    length = ids.shape[1]
    ids_col = jnp.broadcast_to(ids.reshape(-1, 1), (length, LANES))
    tables = (cosine, sine, jnp.broadcast_to(ids, (8, length)), ids_col)

    normed_one, scale_one = moments(rows_in)
    low_own = (normed_one * gain_one).astype(BF16)
    low_one = jnp.concatenate([low_own, swap(low_own, "c")], axis=0)
    qkv_parts = plane_gather(qkv_own)
    rest_parts = plane_gather(rest_own)
    saved = [attention(low_one, part, tables) for part in qkv_parts]
    own, other = partial_rows([item[3] for item in saved], rest_parts)
    hidden = rows_in + own + swap(other, "c").astype(F32)
    normed_two, scale_two = moments(hidden)
    low_own = (normed_two * gain_two).astype(BF16)
    low_two = jnp.concatenate([low_own, swap(low_own, "c")], axis=0)

    sums = None
    rest_grads = []
    for part in rest_parts:
        sums, grads = mlp(low_two, dy, part, sums)
        rest_grads.append(grads)
    half = 2 * piece
    result = hidden + sums[0][:half] + swap(sums[0][half:].astype(BF16), "c").astype(F32)
    output = from_sequence(result.astype(BF16), straight, x)
    dn_two = sums[1][:half] + swap(sums[1][half:].astype(BF16), "c").astype(F32)
    pulled, gain_grad_two = norm_back(dn_two, gain_two, normed_two, scale_two)
    grad_hidden = dy_own.astype(F32) + pulled
    branch_own = grad_hidden.astype(BF16)
    branch = jnp.concatenate([branch_own, swap(branch_own, "c")], axis=0)
    rest_total = plane_reduce(rest_grads)
    rest_owned = owned_gradient(jnp.concatenate(rest_total, axis=0), c)

    mixed_grads, qkv_grads = [None] * 4, [None] * 4
    for r in (3, 1, 2, 0):
        mixed_grads[r], low, high = attention_back(saved[r], branch, low_one, rest_parts[r], tables)
        qkv_grads[r] = (low, high)
    own, other = partial_rows(mixed_grads, qkv_parts)
    dn_one = own + swap(other, "c").astype(F32)
    pulled, gain_grad_one = norm_back(dn_one, gain_one, normed_one, scale_one)
    input_grad = from_sequence((grad_hidden + pulled).astype(BF16), straight, x)
    gain_rows = jnp.stack([gain_grad_one, gain_grad_two]).reshape(2, -1, LANES).transpose(1, 0, 2)
    gain_rows = jnp.pad(gain_rows, ((0, 0), (0, 6), (0, 0))).astype(BF16)
    qkv_total = jnp.concatenate(plane_reduce(qkv_grads), axis=0)
    qkv_owned = owned_gradient(jnp.concatenate([qkv_total, gain_rows], axis=1), c)

    rest_all = in_order(rest_owned, x, y, c).astype(F32)
    blocks = rest_all.reshape(4, 2, 3, HIDDEN, LANES)[:, :, :, :UNITS].transpose(2, 1, 0, 3, 4)
    grad_in = blocks[0:2].reshape(2 * FF, LANES).T
    grad_down = blocks[2].reshape(FF, LANES)
    qkv_all = in_order(qkv_owned, x, y, c).astype(F32)
    qk = qkv_all[:, :, : 2 * OUT].reshape(4, 2, 2, 2, PAIR, HALF, LANES).transpose(6, 1, 0, 4, 2, 3, 5)
    val = qkv_all[:, :, 2 * OUT : QKV].reshape(4, 2, PAIR, 2, HALF, LANES).transpose(5, 1, 0, 2, 3, 4)
    grad_qkv = jnp.concatenate([qk, val[:, :, :, :, None]], axis=4).reshape(LANES, 3 * HEADS * HD)
    grad_out = qkv_all[:, :, QKV : QKV + OUT].transpose(1, 0, 2, 3).reshape(HEADS * HD, LANES)
    gain_sums = jnp.sum(qkv_all[:, :, QKV + OUT : QKV + OUT + 2], axis=(0, 1))
    return output, input_grad, grad_qkv, grad_out, grad_in, grad_down, gain_sums[0], gain_sums[1]


def solution(mesh):
    columns, pieces = mesh.shape["fsdp"], mesh.shape["seq"]
    if pieces != 4 or columns * LANES != D:
        return spread(mesh)
    chips = Mesh(mesh.devices.reshape(columns // 2, 2, 2, 2), ("z", "c", "y", "x"))
    batch, width, seq = ("z", "c"), ("z", "c"), ("y", "x")
    return jax.shard_map(
        chip_local,
        mesh=chips,
        in_specs=(
            P(batch, seq, None),
            P(batch, seq),
            P(width, None),
            P(None, width),
            P(width, None),
            P(None, width),
            P(width),
            P(width),
            P(batch, seq, None),
        ),
        out_specs=(
            P(batch, seq, None),
            P(batch, seq, None),
            P(width, None),
            P(None, width),
            P(width, None),
            P(None, width),
            P(width),
            P(width),
        ),
        check_vma=False,
    )
```

```python
import functools
import math

import jax
import jax.numpy as jnp
from jax import lax
from jax.experimental import pallas as pl
from jax.experimental.pallas import tpu as pltpu
from jax.sharding import Mesh
from jax.sharding import PartitionSpec as P

D = 1024
HEADS = 16
HD = 64
FF = 2624
SEQ_MB = 1
MICRO = 2


def normalize(rows_in, gain):
    center_of = jnp.mean(rows_in, axis=-1, keepdims=True)
    centered = rows_in - center_of
    spread = jnp.mean(centered * centered, axis=-1, keepdims=True)
    return centered * lax.rsqrt(spread + 1e-05) * gain


def doc_positions(seg_rows):
    places = jnp.arange(seg_rows.shape[1], dtype=jnp.int32)[None, :]
    before = jnp.concatenate([seg_rows[:, :1] - 1, seg_rows[:, :-1]], axis=1)
    begins = jnp.where(seg_rows != before, places, 0)
    return places - lax.cummax(begins, axis=1)


def rope_tables(positions, head_dim):
    half_dim = head_dim // 2
    inverse = jnp.exp(
        jnp.arange(half_dim, dtype=jnp.float32) * (-2.0 * math.log(160000.0) / head_dim)
    )
    angles = positions.astype(jnp.float32)[..., None] * inverse
    return (jnp.cos(angles), jnp.sin(angles))


def rotate(vector, cosine, sine):
    half_dim = vector.shape[-1] // 2
    first, second = (vector[..., :half_dim], vector[..., half_dim:])
    return jnp.concatenate(
        [first * cosine - second * sine, second * cosine + first * sine], axis=-1
    )


def gelu_mix(gate_part, up_part):
    return jax.nn.gelu(gate_part, approximate=False) * up_part


def contract_rows(left, right):
    return lax.dot_general(
        left, right, (((0,), (0,)), ((), ())), preferred_element_type=jnp.float32
    )


def contract_cols(left, right):
    return lax.dot_general(
        left, right, (((1,), (1,)), ((), ())), preferred_element_type=jnp.float32
    )


def fetch(w_qkv, w_out, w_in, w_down, gain_attn, gain_mlp):
    return (
        lax.all_gather(w_qkv, "fsdp", axis=0, tiled=True),
        lax.all_gather(w_out, "fsdp", axis=1, tiled=True),
        lax.all_gather(w_in, "fsdp", axis=0, tiled=True),
        lax.all_gather(w_down, "fsdp", axis=1, tiled=True),
        lax.all_gather(gain_attn, "fsdp", axis=0, tiled=True),
        lax.all_gather(gain_mlp, "fsdp", axis=0, tiled=True),
    )


def attend_forward(queries, key_rows, values, seg_rows, block_rows):
    row_count, length, head_count, head_dim = queries.shape
    scaling = 1.0 / math.sqrt(head_dim)

    def advance(number, carried):
        out_buffer, sums_buffer = carried
        offset = number * block_rows
        query_block = lax.dynamic_slice_in_dim(queries, offset, block_rows, 1)
        seg_block = lax.dynamic_slice_in_dim(seg_rows, offset, block_rows, 1)
        scores = (
            jnp.einsum("rqhd,rkhd->rhqk", query_block, key_rows, preferred_element_type=jnp.float32)
            * scaling
        )
        allowed = seg_block[:, None, :, None] == seg_rows[:, None, None, :]
        scores = jnp.where(allowed, scores, -1e30)
        highest = jnp.max(scores, axis=-1, keepdims=True)
        raised = jnp.exp(scores - highest)
        totals = jnp.sum(raised, axis=-1, keepdims=True)
        shares = (raised / totals).astype(jnp.bfloat16)
        out_block = jnp.einsum(
            "rhqk,rkhd->rqhd", shares, values, preferred_element_type=jnp.float32
        )
        log_block = (highest + jnp.log(totals))[..., 0]
        out_buffer = lax.dynamic_update_slice_in_dim(
            out_buffer, out_block.astype(jnp.bfloat16), offset, 1
        )
        sums_buffer = lax.dynamic_update_slice_in_dim(sums_buffer, log_block, offset, 2)
        return (out_buffer, sums_buffer)

    initial = (
        jnp.zeros(queries.shape, jnp.bfloat16),
        jnp.zeros((row_count, head_count, length), jnp.float32),
    )
    return lax.fori_loop(0, length // block_rows, advance, initial)


def attend_backward(queries, key_rows, values, seg_rows, log_sums, grad_context, block_rows):
    row_count, length, head_count, head_dim = queries.shape
    scaling = 1.0 / math.sqrt(head_dim)

    def advance(number, carried):
        grad_query, grad_key, grad_value = carried
        offset = number * block_rows
        query_block = lax.dynamic_slice_in_dim(queries, offset, block_rows, 1)
        seg_block = lax.dynamic_slice_in_dim(seg_rows, offset, block_rows, 1)
        grad_block = lax.dynamic_slice_in_dim(grad_context, offset, block_rows, 1)
        sums_block = lax.dynamic_slice_in_dim(log_sums, offset, block_rows, 2)
        scores = (
            jnp.einsum("rqhd,rkhd->rhqk", query_block, key_rows, preferred_element_type=jnp.float32)
            * scaling
        )
        allowed = seg_block[:, None, :, None] == seg_rows[:, None, None, :]
        shares = jnp.where(allowed, jnp.exp(scores - sums_block[..., None]), 0.0)
        grad_value = grad_value + jnp.einsum(
            "rhqk,rqhd->rkhd",
            shares.astype(jnp.bfloat16),
            grad_block,
            preferred_element_type=jnp.float32,
        )
        grad_shares = jnp.einsum(
            "rqhd,rkhd->rhqk", grad_block, values, preferred_element_type=jnp.float32
        )
        grad_scores = shares * (grad_shares - jnp.sum(shares * grad_shares, axis=-1, keepdims=True))
        rounded = grad_scores.astype(jnp.bfloat16)
        query_piece = (
            jnp.einsum("rhqk,rkhd->rqhd", rounded, key_rows, preferred_element_type=jnp.float32)
            * scaling
        )
        grad_key = (
            grad_key
            + jnp.einsum(
                "rhqk,rqhd->rkhd", rounded, query_block, preferred_element_type=jnp.float32
            )
            * scaling
        )
        grad_query = lax.dynamic_update_slice_in_dim(
            grad_query, query_piece.astype(jnp.bfloat16), offset, 1
        )
        return (grad_query, grad_key, grad_value)

    initial = (
        jnp.zeros(queries.shape, jnp.bfloat16),
        jnp.zeros(queries.shape, jnp.float32),
        jnp.zeros(queries.shape, jnp.float32),
    )
    grad_query, grad_key, grad_value = lax.fori_loop(0, length // block_rows, advance, initial)
    return (grad_query, grad_key.astype(jnp.bfloat16), grad_value.astype(jnp.bfloat16))


def zero_totals():
    return (
        jnp.zeros((D, 3 * HEADS * HD), jnp.float32),
        jnp.zeros((HEADS * HD, D), jnp.float32),
        jnp.zeros((D, 2 * FF), jnp.float32),
        jnp.zeros((FF, D), jnp.float32),
        jnp.zeros((D,), jnp.float32),
        jnp.zeros((D,), jnp.float32),
    )


def local(tokens, segment_ids, w_qkv, w_out, w_in, w_down, gain_attn, gain_mlp, grad_output):
    seq_devices = lax.axis_size("seq")
    piece_len = tokens.shape[1]
    local_heads = HEADS // seq_devices
    all_ids = lax.all_gather(segment_ids, "seq", axis=1, tiled=True)
    length = all_ids.shape[1]
    block_rows = min(512, length)
    all_positions = doc_positions(all_ids)
    own_positions = lax.dynamic_slice_in_dim(
        all_positions, lax.axis_index("seq") * piece_len, piece_len, 1
    )
    acc_qkv, acc_out, acc_in, acc_down, acc_gain_attn, acc_gain_mlp = zero_totals()
    outputs = []
    input_grads = []
    per_micro = SEQ_MB
    for micro_index in range(MICRO):
        lower = micro_index * per_micro
        upper = lower + per_micro
        gathered = fetch(w_qkv, w_out, w_in, w_down, gain_attn, gain_mlp)
        full_qkv, full_out, full_in, full_down, full_gain_attn, full_gain_mlp = gathered
        gain_one = full_gain_attn.astype(jnp.float32)
        gain_two = full_gain_mlp.astype(jnp.float32)
        rows_in = tokens[lower:upper].astype(jnp.float32).reshape(-1, D)
        low_one = normalize(rows_in, gain_one).astype(jnp.bfloat16)
        mixed = jnp.dot(low_one, full_qkv, preferred_element_type=jnp.float32).reshape(
            per_micro, piece_len, HEADS, 3, HD
        )
        cosine, sine = rope_tables(own_positions[lower:upper], HD)
        cosine = cosine[:, :, None, :]
        sine = sine[:, :, None, :]
        stacked = jnp.stack(
            [
                rotate(mixed[:, :, :, 0], cosine, sine),
                rotate(mixed[:, :, :, 1], cosine, sine),
                mixed[:, :, :, 2],
            ],
            axis=3,
        )
        stacked = stacked.astype(jnp.bfloat16).reshape(per_micro, piece_len, HEADS * 3 * HD)
        head_side = lax.all_to_all(stacked, "seq", split_axis=2, concat_axis=1, tiled=True).reshape(
            per_micro, length, local_heads, 3, HD
        )
        queries = head_side[:, :, :, 0]
        key_rows = head_side[:, :, :, 1]
        values = head_side[:, :, :, 2]
        ids_micro = all_ids[lower:upper]
        attended, log_sums = attend_forward(queries, key_rows, values, ids_micro, block_rows)
        token_side = lax.all_to_all(
            attended.reshape(per_micro, length, local_heads * HD),
            "seq",
            split_axis=1,
            concat_axis=2,
            tiled=True,
        )
        context = token_side.reshape(-1, HEADS * HD)
        hidden = rows_in + jnp.dot(context, full_out, preferred_element_type=jnp.float32)
        low_two = normalize(hidden, gain_two).astype(jnp.bfloat16)
        gate_up = jnp.dot(low_two, full_in, preferred_element_type=jnp.float32)
        gate_part = gate_up[:, :FF]
        up_part = gate_up[:, FF:]
        product = gelu_mix(gate_part, up_part).astype(jnp.bfloat16)
        result = hidden + jnp.dot(product, full_down, preferred_element_type=jnp.float32)
        outputs.append(result.astype(jnp.bfloat16).reshape(per_micro, piece_len, D))
        grad_rows = grad_output[lower:upper].reshape(-1, D)
        acc_down = acc_down + contract_rows(product, grad_rows)
        grad_product = contract_cols(grad_rows, full_down)
        unused_mix, pull_mix = jax.vjp(gelu_mix, gate_part, up_part)
        grad_gate, grad_up = pull_mix(grad_product)
        grad_gate_up = jnp.concatenate([grad_gate, grad_up], axis=1).astype(jnp.bfloat16)
        acc_in = acc_in + contract_rows(low_two, grad_gate_up)
        grad_normed_two = contract_cols(grad_gate_up, full_in)
        unused_two, pull_two = jax.vjp(normalize, hidden, gain_two)
        grad_hidden_part, grad_gain_two = pull_two(grad_normed_two)
        acc_gain_mlp = acc_gain_mlp + grad_gain_two
        grad_hidden = grad_rows.astype(jnp.float32) + grad_hidden_part
        grad_branch = grad_hidden.astype(jnp.bfloat16)
        acc_out = acc_out + contract_rows(context, grad_branch)
        grad_context = (
            contract_cols(grad_branch, full_out)
            .astype(jnp.bfloat16)
            .reshape(per_micro, piece_len, HEADS * HD)
        )
        grad_heads = lax.all_to_all(
            grad_context, "seq", split_axis=2, concat_axis=1, tiled=True
        ).reshape(per_micro, length, local_heads, HD)
        grad_query, grad_key, grad_value = attend_backward(
            queries, key_rows, values, ids_micro, log_sums, grad_heads, block_rows
        )
        grad_stack = jnp.stack([grad_query, grad_key, grad_value], axis=3).reshape(
            per_micro, length, local_heads * 3 * HD
        )
        grad_tok_side = (
            lax.all_to_all(grad_stack, "seq", split_axis=1, concat_axis=2, tiled=True)
            .reshape(per_micro, piece_len, HEADS, 3, HD)
            .astype(jnp.float32)
        )
        grad_mixed = jnp.stack(
            [
                rotate(grad_tok_side[:, :, :, 0], cosine, -sine),
                rotate(grad_tok_side[:, :, :, 1], cosine, -sine),
                grad_tok_side[:, :, :, 2],
            ],
            axis=3,
        )
        grad_mixed = grad_mixed.astype(jnp.bfloat16).reshape(-1, 3 * HEADS * HD)
        acc_qkv = acc_qkv + contract_rows(low_one, grad_mixed)
        grad_normed_one = contract_cols(grad_mixed, full_qkv)
        unused_one, pull_one = jax.vjp(normalize, rows_in, gain_one)
        grad_input_part, grad_gain_one = pull_one(grad_normed_one)
        acc_gain_attn = acc_gain_attn + grad_gain_one
        input_grads.append(
            (grad_hidden + grad_input_part).astype(jnp.bfloat16).reshape(per_micro, piece_len, D)
        )
    totals = (acc_qkv, acc_out, acc_in, acc_down, acc_gain_attn, acc_gain_mlp)
    shards = (
        lax.psum_scatter(
            totals[0].astype(jnp.bfloat16), "fsdp", scatter_dimension=0, tiled=True
        ).astype(jnp.float32),
        lax.psum_scatter(
            totals[1].astype(jnp.bfloat16), "fsdp", scatter_dimension=1, tiled=True
        ).astype(jnp.float32),
        lax.psum_scatter(
            totals[2].astype(jnp.bfloat16), "fsdp", scatter_dimension=0, tiled=True
        ).astype(jnp.float32),
        lax.psum_scatter(
            totals[3].astype(jnp.bfloat16), "fsdp", scatter_dimension=1, tiled=True
        ).astype(jnp.float32),
        lax.psum_scatter(
            totals[4].astype(jnp.bfloat16), "fsdp", scatter_dimension=0, tiled=True
        ).astype(jnp.float32),
        lax.psum_scatter(
            totals[5].astype(jnp.bfloat16), "fsdp", scatter_dimension=0, tiled=True
        ).astype(jnp.float32),
    )
    owned = (
        lax.psum(shards[0].astype(jnp.bfloat16), "seq").astype(jnp.float32),
        lax.psum(shards[1].astype(jnp.bfloat16), "seq").astype(jnp.float32),
        lax.psum(shards[2].astype(jnp.bfloat16), "seq").astype(jnp.float32),
        lax.psum(shards[3].astype(jnp.bfloat16), "seq").astype(jnp.float32),
        lax.psum(shards[4].astype(jnp.bfloat16), "seq").astype(jnp.float32),
        lax.psum(shards[5].astype(jnp.bfloat16), "seq").astype(jnp.float32),
    )
    return (
        jnp.concatenate(outputs, axis=0),
        jnp.concatenate(input_grads, axis=0),
        owned[0],
        owned[1],
        owned[2],
        owned[3],
        owned[4],
        owned[5],
    )


def spread(mesh):
    return jax.shard_map(
        local,
        mesh=mesh,
        in_specs=(
            P("fsdp", "seq", None),
            P("fsdp", "seq"),
            P("fsdp", None),
            P(None, "fsdp"),
            P("fsdp", None),
            P(None, "fsdp"),
            P("fsdp"),
            P("fsdp"),
            P("fsdp", "seq", None),
        ),
        out_specs=(
            P("fsdp", "seq", None),
            P("fsdp", "seq", None),
            P("fsdp", None),
            P(None, "fsdp"),
            P("fsdp", None),
            P(None, "fsdp"),
            P("fsdp"),
            P("fsdp"),
        ),
        check_vma=False,
    )


F32 = jnp.float32
BF16 = jnp.bfloat16
NN = (((1,), (0,)), ((), ()))
NT = (((1,), (1,)), ((), ()))
TN = (((0,), (0,)), ((), ()))
MIB = 1 << 20
LANES = 128
HALF = HD // 2
PAIR = 2
QKV = 3 * PAIR * HD
OUT = PAIR * HD
UNITS = FF // 8
HIDDEN = -(-UNITS // 16) * 16
EXTRA = 16
SPLIT = (160, HIDDEN - 160)
TILE = 256
BOTH = [(0, 1), (1, 0)]


def mul(left, right, dims):
    return lax.dot_general(left, right, dims, preferred_element_type=F32)


def whole_in_vmem(count):
    return [pl.BlockSpec(memory_space=pltpu.VMEM)] * count


def after(value, *others):
    return lax.optimization_barrier((value, others))[0]


def lay_flat(flat_ref, blocks_ref, start, count, to=0):
    for k in range(blocks_ref.shape[0]):
        flat_ref[to : to + count, LANES * k : LANES * (k + 1)] = blocks_ref[k, start : start + count, :]


def mlp_body(first, n_ref, dy_ref, wa_ref, wb_ref, *rest):
    if first:
        y_ref, dn_ref, ga_ref, gb_ref, w_all, acc = rest
    else:
        y_in, dn_in, y_ref, dn_ref, ga_ref, gb_ref, w_all, acc = rest
    step = pl.program_id(0)

    @pl.when(step == 0)
    def _():
        for i in range(3):
            lay_flat(w_all, wa_ref, i * SPLIT[0], SPLIT[0], i * HIDDEN)
            lay_flat(w_all, wb_ref, i * SPLIT[1], SPLIT[1], i * HIDDEN + SPLIT[0])

    n_t = n_ref[...]
    dy_t = dy_ref[...]
    gate = mul(w_all[0:HIDDEN, :], n_t, NT)
    up = mul(w_all[HIDDEN : 2 * HIDDEN, :], n_t, NT)
    dm = mul(w_all[2 * HIDDEN :, :], dy_t, NT)
    phi = 0.5 * (1.0 + lax.erf(gate * math.sqrt(0.5)))
    gelu = gate * phi
    slope = phi + gate * (jnp.exp(-0.5 * gate * gate) * (1.0 / math.sqrt(2.0 * math.pi)))
    mix = (gelu * up).astype(BF16)
    dgu = jnp.concatenate([dm * up * slope, dm * gelu], axis=0).astype(BF16)
    y = mul(mix, w_all[2 * HIDDEN :, :], TN)
    dn = mul(dgu, w_all[0 : 2 * HIDDEN, :], TN)
    if first:
        y_ref[...] = y
        dn_ref[...] = dn
    else:
        y_ref[...] = y_in[...] + y
        dn_ref[...] = dn_in[...] + dn
    g_in = mul(dgu, n_t, NN)
    g_down = mul(mix, dy_t, NN)

    @pl.when(step == 0)
    def _():
        acc[0 : 2 * HIDDEN, :] = g_in
        acc[2 * HIDDEN :, :] = g_down

    @pl.when(step != 0)
    def _():
        acc[0 : 2 * HIDDEN, :] += g_in
        acc[2 * HIDDEN :, :] += g_down

    @pl.when(step == pl.num_programs(0) - 1)
    def _():
        half = ga_ref.shape[0]
        for k in range(half):
            ga_ref[k] = acc[:, LANES * k : LANES * (k + 1)].astype(BF16)
            gb_ref[k] = acc[:, LANES * (k + half) : LANES * (k + half + 1)].astype(BF16)


def mlp(n2, dy, weights, sums):
    first = sums is None
    tokens, width = n2.shape
    blocks, _, lanes = weights[0].shape
    row_tile = pl.BlockSpec((TILE, width), lambda t: (t, 0))
    half = pl.BlockSpec((blocks // 2, 3 * HIDDEN, lanes), lambda t: (0, 0, 0))
    total = jax.ShapeDtypeStruct((tokens, width), F32)
    grads = jax.ShapeDtypeStruct((blocks // 2, 3 * HIDDEN, lanes), BF16)
    y, dn, ga, gb = pl.pallas_call(
        functools.partial(mlp_body, first),
        grid=(tokens // TILE,),
        in_specs=[row_tile, row_tile]
        + [pl.BlockSpec(item.shape, lambda t: (0, 0, 0)) for item in weights]
        + ([] if first else [row_tile, row_tile]),
        out_specs=[row_tile, row_tile, half, half],
        out_shape=[total, total, grads, grads],
        scratch_shapes=[pltpu.VMEM((3 * HIDDEN, width), BF16), pltpu.VMEM((3 * HIDDEN, width), F32)],
        input_output_aliases={} if first else {4: 0, 5: 1},
        compiler_params=pltpu.CompilerParams(vmem_limit_bytes=40 * MIB),
        cost_estimate=pl.CostEstimate(
            flops=18 * tokens * HIDDEN * width,
            transcendentals=2 * tokens * HIDDEN,
            bytes_accessed=20 * tokens * width + 12 * HIDDEN * width,
        ),
        name="mlp",
    )(*([n2, dy, *weights] + ([] if first else list(sums))))
    return (y, dn), (ga, gb)


def lane_group(shape, width):
    return (lax.broadcasted_iota(jnp.int32, shape, 1) // width) % 2


def forward_body(n_ref, w_ref, cos_ref, sin_ref, row_ref, col_ref, q_ref, k_ref, v_ref, o_ref, lse_ref, w_all):
    tokens = n_ref.shape[0]
    lay_flat(w_all, w_ref, 0, QKV)

    def project(i, carry):
        here = pl.ds(pl.multiple_of(i * TILE, TILE), TILE)
        mixed = mul(n_ref[here, :], w_all[...], NT)
        cosine, sine = cos_ref[here, :], sin_ref[here, :]
        query, key = mixed[:, 0:OUT], mixed[:, OUT : 2 * OUT]
        q_ref[here, :] = (query * cosine + pltpu.roll(query, HD, 1) * sine).astype(BF16)
        k_ref[here, :] = (key * cosine + pltpu.roll(key, HD, 1) * sine).astype(BF16)
        v_ref[here, :] = mixed[:, 2 * OUT :].astype(BF16)
        return carry

    lax.fori_loop(0, tokens // TILE, project, 0)

    def attend(i, carry):
        here = pl.ds(pl.multiple_of(i * TILE, TILE), TILE)
        query = q_ref[here, :]
        allowed = col_ref[here, 0:1] == row_ref[0:1, :]
        pair = lane_group((TILE, OUT), HALF)
        outs, sums = [], []
        for head in range(PAIR):
            masked = jnp.where(pair == head, query, jnp.zeros_like(query))
            scores = mul(masked, k_ref[...], NT) * (1.0 / math.sqrt(HD))
            scores = jnp.where(allowed, scores, -1e30)
            top = jnp.max(scores, axis=1, keepdims=True)
            raised = jnp.exp(scores - top)
            total = jnp.sum(raised, axis=1, keepdims=True)
            outs.append(mul(raised.astype(BF16), v_ref[...], NN) / total)
            sums.append(top + jnp.log(total))
        side = lane_group((TILE, OUT), HD)
        o_ref[here, :] = jnp.where(side == 0, outs[0], outs[1]).astype(BF16)
        lane = lax.broadcasted_iota(jnp.int32, (TILE, LANES), 1)
        both = jnp.where(lane == 0, sums[0], sums[1])
        lse_ref[:, here] = both.T[0:8, :]
        return carry

    lax.fori_loop(0, tokens // TILE, attend, 0)


def attention(n1, weights, tables):
    tokens, width = n1.shape
    return pl.pallas_call(
        forward_body,
        in_specs=whole_in_vmem(6),
        out_specs=whole_in_vmem(5),
        out_shape=[jax.ShapeDtypeStruct((tokens, OUT), BF16)] * 4 + [jax.ShapeDtypeStruct((8, tokens), F32)],
        scratch_shapes=[pltpu.VMEM((QKV, width), BF16)],
        compiler_params=pltpu.CompilerParams(vmem_limit_bytes=32 * MIB),
        cost_estimate=pl.CostEstimate(
            flops=2 * tokens * QKV * width + 8 * tokens * tokens * OUT,
            transcendentals=2 * tokens * tokens,
            bytes_accessed=6 * MIB,
        ),
        name="attention",
    )(n1, weights, *tables)


def backward_body(
    q_ref, k_ref, v_ref, o_ref, lse_ref, da_ref, n_ref, w_ref, cos_ref, sin_ref, row_ref, col_ref,
    d_ref, ga_ref, gb_ref, w_all, do_ref, dq_ref, dk_ref, dv_ref,
):
    tokens = n_ref.shape[0]
    scaling = 1.0 / math.sqrt(HD)
    lay_flat(w_all, w_ref, 0, OUT)
    do_ref[...] = mul(da_ref[...], w_all[...], NT).astype(BF16)
    dk_ref[...] = jnp.zeros_like(dk_ref)
    dv_ref[...] = jnp.zeros_like(dv_ref)

    def step(i, carry):
        here = pl.ds(pl.multiple_of(i * TILE, TILE), TILE)
        query, grad = q_ref[here, :], do_ref[here, :]
        allowed = col_ref[:, 0:1] == row_ref[0:1, here]
        pair = lane_group((TILE, OUT), HALF)
        side = lane_group((TILE, OUT), HD)
        pair_all = lane_group((tokens, OUT), HALF)
        dq = jnp.zeros((TILE, OUT), F32)
        for head in range(PAIR):
            q_m = jnp.where(pair == head, query, jnp.zeros_like(query))
            g_m = jnp.where(side == head, grad, jnp.zeros_like(grad))
            k_m = jnp.where(pair_all == head, k_ref[...], jnp.zeros_like(k_ref))
            scores = mul(k_ref[...], q_m, NT) * scaling
            share = jnp.exp(jnp.where(allowed, scores - lse_ref[head : head + 1, here], -1e30))
            dshare = mul(v_ref[...], g_m, NT)
            delta = jnp.sum(share * dshare, axis=0, keepdims=True)
            ds = (share * (dshare - delta)).astype(BF16)
            dv_ref[...] += mul(share.astype(BF16), g_m, NN)
            dk_ref[...] += mul(ds, q_m, NN)
            dq += mul(ds, k_m, TN)
        dq_ref[here, :] = dq
        return carry

    lax.fori_loop(0, tokens // TILE, step, 0)
    cosine, sine = cos_ref[...], sin_ref[...]
    dq = (dq_ref[...] * scaling).astype(BF16).astype(F32)
    dk = (dk_ref[...] * scaling).astype(BF16).astype(F32)
    d_ref[:, 0:OUT] = (dq * cosine - pltpu.roll(dq, HD, 1) * sine).astype(BF16)
    d_ref[:, OUT : 2 * OUT] = (dk * cosine - pltpu.roll(dk, HD, 1) * sine).astype(BF16)
    d_ref[:, 2 * OUT :] = dv_ref[...].astype(BF16)
    half = ga_ref.shape[0]
    for k in range(half):
        for ref, at in ((ga_ref, k), (gb_ref, k + half)):
            lanes = slice(LANES * at, LANES * (at + 1))
            ref[k, 0:QKV, :] = mul(d_ref[...], n_ref[:, lanes], TN).astype(BF16)
            ref[k, QKV:, :] = mul(o_ref[...], da_ref[:, lanes], TN).astype(BF16)


def attention_back(saved, dattn, n1, rest, tables):
    tokens, width = n1.shape
    blocks = rest.shape[0]
    vmem = pl.BlockSpec(memory_space=pltpu.VMEM)
    grads = jax.ShapeDtypeStruct((blocks // 2, QKV + OUT, LANES), BF16)
    return pl.pallas_call(
        backward_body,
        grid=(1,),
        in_specs=[vmem] * 7 + [pl.BlockSpec((blocks, OUT, LANES), lambda i: (0, 0, 0))] + [vmem] * 4,
        out_specs=whole_in_vmem(3),
        out_shape=[jax.ShapeDtypeStruct((tokens, QKV), BF16), grads, grads],
        scratch_shapes=[pltpu.VMEM((OUT, width), BF16), pltpu.VMEM((tokens, OUT), BF16)]
        + [pltpu.VMEM((tokens, OUT), F32)] * 3,
        compiler_params=pltpu.CompilerParams(vmem_limit_bytes=40 * MIB),
        cost_estimate=pl.CostEstimate(
            flops=2 * tokens * width * (QKV + 2 * OUT) + 20 * tokens * tokens * OUT,
            transcendentals=2 * tokens * tokens,
            bytes_accessed=10 * MIB,
        ),
        name="attention_back",
    )(*saved, dattn, n1, rest, *tables)


def gather_body(count, *refs):
    lefts, weights = refs[:count], refs[count : 2 * count]
    own_ref, other_ref, w_all = refs[2 * count :]
    inner = lefts[0].shape[1]
    step = pl.program_id(0)
    steps = pl.num_programs(0)

    @pl.when(step == 0)
    def _():
        for r in range(count):
            lay_flat(w_all, weights[r], 0, inner, r * inner)

    rows = jnp.concatenate([left[...] for left in lefts], axis=1)
    total = mul(rows, w_all[...], NN)

    @pl.when(step < steps // 2)
    def _():
        own_ref[...] = total

    @pl.when(step >= steps // 2)
    def _():
        other_ref[...] = total.astype(BF16)


def partial_rows(lefts, weights):
    count = len(lefts)
    tokens, inner = lefts[0].shape
    blocks = weights[0].shape[0]
    width = blocks * LANES
    steps = tokens // TILE
    return pl.pallas_call(
        functools.partial(gather_body, count),
        grid=(steps,),
        in_specs=[pl.BlockSpec((TILE, inner), lambda t: (t, 0))] * count
        + [pl.BlockSpec((blocks, inner, LANES), lambda t: (0, 0, 0))] * count,
        out_specs=[
            pl.BlockSpec((TILE, width), lambda t: (jnp.minimum(t, steps // 2 - 1), 0)),
            pl.BlockSpec((TILE, width), lambda t: (jnp.maximum(t - steps // 2, 0), 0)),
        ],
        out_shape=[
            jax.ShapeDtypeStruct((tokens // 2, width), F32),
            jax.ShapeDtypeStruct((tokens // 2, width), BF16),
        ],
        scratch_shapes=[pltpu.VMEM((count * inner, width), BF16)],
        compiler_params=pltpu.CompilerParams(vmem_limit_bytes=40 * MIB),
        cost_estimate=pl.CostEstimate(
            flops=2 * tokens * count * inner * width, transcendentals=0, bytes_accessed=8 * MIB
        ),
        name="partial_rows",
    )(*lefts, *weights)


def swap(value, axis):
    return lax.ppermute(value, axis, BOTH)


def plane_pairs():
    near, far = [], []
    for c in range(2):
        for y in range(2):
            for x in range(2):
                at = 4 * c + 2 * y + x
                if c == y:
                    near.append((at, 4 * c + 2 * y + 1 - x))
                else:
                    near.append((at, 4 * y + 2 * (1 - y) + x))
                    far.append((at, 4 * y + 2 * (1 - y) + 1 - x))
    return near, far


def to_sequence(local_rows, straight, x):
    near, far = plane_pairs()
    first, second = local_rows[0], local_rows[1]
    same = jnp.where(x == 0, first, second)
    other = jnp.where(x == 0, second, first)
    got_near = lax.ppermute(jnp.where(straight, other, same), ("c", "y", "x"), near)
    got_far = lax.ppermute(other, ("c", "y", "x"), far)
    return jnp.where(straight, same, got_near), jnp.where(straight, got_near, got_far)


def from_sequence(rows, straight, x):
    near, far = plane_pairs()
    piece = rows.shape[0] // 2
    first, second = rows[:piece], rows[piece:]
    got_near = lax.ppermute(jnp.where(straight, second, first), ("c", "y", "x"), near)
    got_far = lax.ppermute(second, ("c", "y", "x"), far)
    same = jnp.where(straight, first, got_near)
    other = jnp.where(straight, got_near, got_far)
    return jnp.where(x == 0, jnp.stack([same, other]), jnp.stack([other, same]))


def moments(rows):
    center = jnp.mean(rows, axis=-1, keepdims=True)
    shifted = rows - center
    scale = lax.rsqrt(jnp.mean(shifted * shifted, axis=-1, keepdims=True) + 1e-05)
    return shifted * scale, scale


def norm_back(grad, gain, normed, scale):
    scaled = grad * gain
    pulled = scaled - jnp.mean(scaled, axis=-1, keepdims=True)
    pulled = pulled - normed * jnp.mean(scaled * normed, axis=-1, keepdims=True)
    return pulled * scale


def corner_half(value, part, axis):
    half = value.shape[0] // 2
    return swap(value[part * half : (part + 1) * half], axis)


def swap_corner(value):
    return lax.ppermute(value, ("y", "x"), [(0, 3), (1, 2), (2, 1), (3, 0)])


def add_low(left, right):
    return (left.astype(F32) + right.astype(F32)).astype(BF16)


def where_from(places_ref, r, h):
    core = places_ref[0] if h == 0 else 1 - places_ref[0]
    row = places_ref[1] if r < 2 else 1 - places_ref[1]
    column = places_ref[2] if r % 2 == 0 else 1 - places_ref[2]
    return core, 2 * row + column


def gain_gradient(pairs, gain_ref, out_ref):
    total = jnp.zeros((LANES, LANES), F32)
    for weight, grad in pairs:
        total += weight.astype(F32) * grad
    out_ref[...] = jnp.sum(total.T, axis=0, keepdims=True) / gain_ref[...]


def rest_order_body(places_ref, *refs):
    parts, (w_ref, gain_ref, in_ref, down_ref, gain_grad_ref, rows) = refs[:4], refs[4:]
    for r in range(4):
        for h in range(2):
            core, place = where_from(places_ref, r, h)
            at = pl.multiple_of((core * 4 + place) * UNITS, 8)
            for i in range(2):
                rows[pl.ds(i * FF + at, UNITS), :] = parts[r][h, i * HIDDEN : (i + 1) * HIDDEN].astype(F32)[:UNITS]
            down_ref[pl.ds(at, UNITS), :] = parts[r][h, 2 * HIDDEN :].astype(F32)[:UNITS]
    turned_pairs(rows, in_ref, w_ref, gain_ref, gain_grad_ref)


def turned_pairs(rows, grad_ref, w_ref, gain_ref, gain_grad_ref):
    pairs = []
    for j in range(grad_ref.shape[1] // LANES):
        lanes = slice(LANES * j, LANES * (j + 1))
        grad = rows[lanes, :].T
        grad_ref[:, lanes] = grad
        pairs.append((w_ref[:, lanes], grad))
    gain_gradient(pairs, gain_ref, gain_grad_ref)


def qkv_order_body(places_ref, *refs):
    parts, (w_ref, gain_ref, qkv_ref, out_ref, gain_grad_ref, rows) = refs[:4], refs[4:]
    for r in range(4):
        for h in range(2):
            core, place = where_from(places_ref, r, h)
            part = parts[r][h].astype(F32)
            at = (core * 4 + place) * QKV
            for head in range(PAIR):
                for t in range(2):
                    for side in range(2):
                        to = pl.multiple_of(at + head * 3 * HD + t * HD + side * HALF, 8)
                        source = t * OUT + side * HD + head * HALF
                        rows[pl.ds(to, HALF), :] = part[source : source + HALF]
                to = pl.multiple_of(at + head * 3 * HD + 2 * HD, 8)
                rows[pl.ds(to, HD), :] = part[2 * OUT + head * HD : 2 * OUT + (head + 1) * HD]
            to = pl.multiple_of((core * 4 + place) * OUT, 8)
            out_ref[pl.ds(to, OUT), :] = part[QKV : QKV + OUT]
    turned_pairs(rows, qkv_ref, w_ref, gain_ref, gain_grad_ref)


def in_weight_order(body, places, parts, weight, gain, shapes, rows, name):
    return pl.pallas_call(
        body,
        in_specs=[pl.BlockSpec(memory_space=pltpu.SMEM)] + whole_in_vmem(6),
        out_specs=whole_in_vmem(len(shapes)),
        out_shape=[jax.ShapeDtypeStruct(shape, F32) for shape in shapes],
        scratch_shapes=[pltpu.VMEM((rows, LANES), F32)],
        compiler_params=pltpu.CompilerParams(vmem_limit_bytes=24 * MIB),
        cost_estimate=pl.CostEstimate(flops=0, transcendentals=0, bytes_accessed=16 * rows * LANES),
        name=name,
    )(places, *parts, weight, gain.astype(F32).reshape(1, LANES))


def owned_gradient(mine, c):
    keep = lax.dynamic_index_in_dim(mine, c, 0, keepdims=False)
    give = lax.dynamic_index_in_dim(mine, 1 - c, 0, keepdims=False)
    own = jnp.stack([keep, swap(give, "c")])
    return [own, swap(own, "x"), swap(own, "y"), swap_corner(own)]


def core_pieces(pieces, c):
    keep = lax.dynamic_index_in_dim(pieces, c, 0, keepdims=False)
    give = lax.dynamic_index_in_dim(pieces, 1 - c, 0, keepdims=False)
    got = swap(give, "c")
    return jnp.where(c == 0, jnp.stack([keep, got]), jnp.stack([got, keep]))


def gather_columns(pieces):
    return lax.all_gather(pieces, "z", axis=0, tiled=True)


def chip_local(tokens, segment_ids, w_qkv, w_out, w_in, w_down, gain_attn, gain_mlp, grad_output):
    c, y, x = lax.axis_index("c"), lax.axis_index("y"), lax.axis_index("x")
    place = 2 * y + x
    straight = c == y
    piece = tokens.shape[1]

    qkv = lax.dynamic_index_in_dim(w_qkv.reshape(LANES, 2, 4, QKV), place, 2, keepdims=False)
    qkv = qkv.reshape(LANES, 2, PAIR, 3, 2, HALF)
    qk = qkv[:, :, :, 0:2].transpose(1, 3, 4, 2, 5, 0).reshape(2, 2 * OUT, LANES)
    val = qkv[:, :, :, 2].transpose(1, 2, 3, 4, 0).reshape(2, OUT, LANES)
    gains = jnp.broadcast_to(jnp.stack([gain_attn, gain_mlp])[None], (2, 2, LANES))
    gains = jnp.concatenate([gains, jnp.zeros((2, EXTRA - 2, LANES), BF16)], axis=1)
    first_pieces = jnp.concatenate([qk, val, gains], axis=1)
    out_rows = lax.dynamic_index_in_dim(w_out.reshape(2, 4, OUT, LANES), place, 1, keepdims=False)
    down_rows = lax.dynamic_index_in_dim(w_down.reshape(2, 4, UNITS, LANES), place, 1, keepdims=False)
    in_rows = lax.dynamic_index_in_dim(w_in.T.reshape(2, 2, 4, UNITS, LANES), place, 2, keepdims=False)
    units = [in_rows[0], in_rows[1], down_rows]
    fill = ((0, 0), (0, HIDDEN - UNITS), (0, 0))
    early = jnp.concatenate([out_rows] + [item[:, : SPLIT[0]] for item in units], axis=1)
    late = jnp.concatenate([jnp.pad(item[:, SPLIT[0] :], fill) for item in units], axis=1)
    qkv_own = gather_columns(core_pieces(first_pieces, c))
    others = core_pieces(jnp.concatenate([early, late], axis=1), c)
    early_own = gather_columns(after(others[:, : early.shape[1]], qkv_own))
    gain_one = qkv_own[:, QKV, :].reshape(1, D).astype(F32)
    gain_two = qkv_own[:, QKV + 1, :].reshape(1, D).astype(F32)

    ids_row = jnp.pad(segment_ids.astype(BF16)[:, None, :], ((0, 0), (0, 7), (0, D - piece)))
    first, second = to_sequence(jnp.concatenate([tokens, ids_row], axis=1), straight, x)
    rows_in = jnp.concatenate([first[:piece], second[:piece]], axis=0).astype(F32)
    own_ids = jnp.concatenate([first[piece : piece + 1, :piece], second[piece : piece + 1, :piece]], axis=1)
    ids = jnp.concatenate([own_ids, swap(own_ids, "c")], axis=1).astype(F32)
    dy_first, dy_second = to_sequence(grad_output, straight, x)
    dy_own = jnp.concatenate([dy_first, dy_second], axis=0)
    dy = jnp.concatenate([dy_own, swap(dy_own, "c")], axis=0)

    order = jnp.stack([2 * c + x, 2 * c + 1 - x, 2 * (1 - c) + x, 2 * (1 - c) + 1 - x])
    places = (order[:, None] * piece + jnp.arange(piece)[None, :]).reshape(-1)
    begins = jnp.sum((ids < ids.reshape(-1, 1)).astype(F32), axis=1)
    cosine, sine = rope_tables(places.astype(F32) - begins, HD)
    cosine = jnp.concatenate([cosine] * 4, axis=1)
    sine = jnp.concatenate([-sine, -sine, sine, sine], axis=1)
    length = ids.shape[1]
    ids_col = jnp.broadcast_to(ids.reshape(-1, 1), (length, LANES))
    tables = (cosine, sine, jnp.broadcast_to(ids, (8, length)), ids_col)

    normed_one, scale_one = moments(rows_in)
    low_own = (normed_one * gain_one).astype(BF16)
    low_one = jnp.concatenate([low_own, swap(low_own, "c")], axis=0)
    qkv_parts = [qkv_own, swap(qkv_own, "x"), swap(qkv_own, "y")]
    saved = [attention(low_one, qkv_own, tables)]
    across, along = after(tuple(qkv_parts[1:]), saved[0][3])
    corner = [corner_half(along, 0, "x"), corner_half(across, 1, "y")]
    late_own = gather_columns(after(others[:, early.shape[1] :], saved[0][3]))
    saved.append(attention(after(low_one, saved[0][3], across, along, dy), across, tables))
    early_own = after(early_own, saved[1][3])
    out_own, early_own = early_own[:, :OUT], early_own[:, OUT:]
    out_parts = [out_own, swap(out_own, "x"), swap(out_own, "y"), swap_corner(out_own)]
    early_parts = [early_own, swap(early_own, "x"), swap(early_own, "y")]
    saved.append(attention(after(low_one, saved[1][3], early_own), along, tables))
    qkv_parts.append(jnp.concatenate(corner, axis=0))
    saved.append(attention(after(low_one, saved[2][3]), qkv_parts[3], tables))
    late_own = after(late_own, saved[3][3])
    late_parts = [late_own, swap(late_own, "x"), swap(late_own, "y")]
    own, other = partial_rows([item[3] for item in saved], out_parts)
    hidden = rows_in + own + swap(other, "c").astype(F32)
    normed_two, scale_two = moments(hidden)
    low_own = (normed_two * gain_two).astype(BF16)
    low_two = jnp.concatenate([low_own, swap(low_own, "c")], axis=0)

    grads, got = [None] * 4, {}
    across, along = after(tuple(early_parts[1:]), low_own)
    early_corner = [corner_half(along, 0, "x"), corner_half(across, 1, "y")]
    sums, grads[0] = mlp(after(low_two, across, along), dy, (early_own, late_own), None)
    across, along = after(tuple(late_parts[1:]), sums)
    late_corner = [corner_half(along, 0, "x"), corner_half(across, 1, "y")]
    sums, grads[1] = mlp(after(low_two, across, along), dy, (early_parts[1], across), sums)
    got[1, 0] = swap(grads[1][0], "x")
    sums, grads[2] = mlp(low_two, dy, (early_parts[2], along), sums)
    got[2, 1] = swap(grads[2][1], "y")
    early_corner, late_corner = after((tuple(early_corner), tuple(late_corner)), sums)
    corner = (jnp.concatenate(early_corner, axis=0), jnp.concatenate(late_corner, axis=0))
    sums, grads[3] = mlp(after(low_two, got[1, 0]), dy, corner, sums)
    got[3, 0], got[3, 1] = swap(grads[3][0], "x"), swap(grads[3][1], "y")
    half = 2 * piece
    dn_two = sums[1][:half] + swap(after(sums[1][half:].astype(BF16), got[2, 1]), "c").astype(F32)
    result = hidden + sums[0][:half] + swap(sums[0][half:].astype(BF16), "c").astype(F32)
    pulled = norm_back(dn_two, gain_two, normed_two, scale_two)
    grad_hidden = dy_own.astype(F32) + pulled
    branch_own = grad_hidden.astype(BF16)
    branch = jnp.concatenate([branch_own, swap(branch_own, "c")], axis=0)

    mixed_grads, qkv_grads, q_got = [None] * 4, [None] * 4, {}

    def back(r, *others):
        mixed_grads[r], low, high = attention_back(saved[r], after(branch, *others), low_one, out_parts[r], tables)
        qkv_grads[r] = (low, high)

    def summed(r, h, piece, done):
        return add_low(grads[r][h], after(piece, done))

    back(3)
    done = mixed_grads[3]
    here_a, next_a = summed(0, 0, got[1, 0], done), summed(2, 0, got[3, 0], done)
    here_b, next_b = summed(0, 1, got[2, 1], done), summed(1, 1, got[3, 1], done)
    got_a, got_b = swap(next_a, "y"), swap(next_b, "x")
    back(1, here_a, next_a, here_b, next_b)
    done = mixed_grads[1]
    low, high = after(qkv_grads[3], done)
    q_got[3, 0], q_got[3, 1] = swap(low, "x"), swap(high, "y")
    q_got[1, 0] = swap(qkv_grads[1][0], "x")
    back(2, done)
    done = mixed_grads[2]
    q_got[2, 1] = swap(qkv_grads[2][1], "y")
    got_a, got_b = after((got_a, got_b), done)
    rest_total = jnp.concatenate([add_low(here_a, got_a), add_low(here_b, got_b)], axis=0)
    rest_sum = lax.psum_scatter(rest_total, "z", scatter_dimension=0, tiled=True)
    next_a = add_low(qkv_grads[2][0], after(q_got[3, 0], done))
    next_b = add_low(qkv_grads[1][1], after(q_got[3, 1], done))
    got_a, got_b = swap(next_a, "y"), swap(next_b, "x")
    back(0, rest_total, q_got[1, 0], next_a, next_b)
    done = mixed_grads[0]
    here_a = add_low(qkv_grads[0][0], q_got[1, 0])
    here_b = add_low(qkv_grads[0][1], after(q_got[2, 1], done))
    got_a, got_b = after((got_a, got_b), done)
    qkv_total = jnp.concatenate([add_low(here_a, got_a), add_low(here_b, got_b)], axis=0)
    qkv_sum = lax.psum_scatter(after(qkv_total, rest_sum), "z", scatter_dimension=0, tiled=True)
    rest_owned = owned_gradient(rest_sum, c)
    own, other = partial_rows(after(tuple(mixed_grads), qkv_total), qkv_parts)
    dn_one = own + swap(other, "c").astype(F32)
    input_grad = (grad_hidden + norm_back(dn_one, gain_one, normed_one, scale_one)).astype(BF16)
    output = from_sequence(after(result.astype(BF16), own), straight, x)
    input_grad = from_sequence(input_grad, straight, x)
    qkv_owned = owned_gradient(qkv_sum, c)

    own_place = jnp.stack([c, y, x]).astype(jnp.int32)
    grad_in, grad_down, grad_gain_mlp = in_weight_order(
        rest_order_body,
        own_place,
        rest_owned,
        w_in,
        gain_mlp,
        [(LANES, 2 * FF), (FF, LANES), (1, LANES)],
        2 * FF,
        "rest_order",
    )
    grad_qkv, grad_out, grad_gain_attn = in_weight_order(
        qkv_order_body,
        own_place,
        qkv_owned,
        w_qkv,
        gain_attn,
        [(LANES, 3 * HEADS * HD), (HEADS * HD, LANES), (1, LANES)],
        3 * HEADS * HD,
        "qkv_order",
    )
    gain_grads = grad_gain_attn.reshape(-1), grad_gain_mlp.reshape(-1)
    return output, input_grad, grad_qkv, grad_out, grad_in, grad_down, *gain_grads


def solution(mesh):
    columns, pieces = mesh.shape["fsdp"], mesh.shape["seq"]
    if pieces != 4 or columns * LANES != D:
        return spread(mesh)
    chips = Mesh(mesh.devices.reshape(columns // 2, 2, 2, 2), ("z", "c", "y", "x"))
    batch, width, seq = ("z", "c"), ("z", "c"), ("y", "x")
    return jax.shard_map(
        chip_local,
        mesh=chips,
        in_specs=(
            P(batch, seq, None),
            P(batch, seq),
            P(width, None),
            P(None, width),
            P(width, None),
            P(None, width),
            P(width),
            P(width),
            P(batch, seq, None),
        ),
        out_specs=(
            P(batch, seq, None),
            P(batch, seq, None),
            P(width, None),
            P(None, width),
            P(width, None),
            P(None, width),
            P(width),
            P(width),
        ),
        check_vma=False,
    )
```
